1024 devices in a mesh: cells: 128 (over y, z), orb: 8 (over x, core).
Axes of the slice: x: 4, y: 4, z: 32, core: 2. Of those that a mesh axis runs over, the one named last changes fastest.
Arguments:
- initial: float32 [512, 65536], P('orb', 'cells'), may hold values from -500 to 500, as said below
- cell_matrices: float32 [128, 512, 512], P('cells'), may hold values from -0.22097087 to 0.22097087, as said below
- cell_map: int32 [128, 512], P('cells'), may hold values from 0 to 511, as said below
- face_low: int32 [128, 64], P('cells'), may hold values from 0 to 511, as said below
- face_high: int32 [128, 64], P('cells'), may hold values from 0 to 511, as said below
Outputs:
- orbitals: float32 [512, 65536], P('orb', 'cells')
The draws below stay inside these ranges and needn't reach their ends.
Inputs may be any that keep to these rules, and one draw needn't show every extreme that they name: `cell_map`: row c holds the device-local numbers of cell c's 512 nodes in the order of cell_matrices' rows; within the 1 cells of one device every number is used, a node belongs to one or two of them. `face_low`: distinct numbers, each in exactly one cell of the device, none also in face_high of the same device; entry k names the same physical node as entry k of face_high of the previous device along the periodic chain. `face_high`: distinct numbers, each in exactly one cell of the device; entry k names the same physical node as entry k of face_low of the next device along the periodic chain. `cell_matrices`: each cell's matrix is symmetric. `initial`: copies of a shared node may differ; only the face_high copy counts.
All inputs are finite; a program needn't handle non-finite values. Where the reference program divides by a largest or mean magnitude, that divisor is 1e-20 or more.
Results may differ from the reference program's by a relative error of at most 0.0003.
Values sent between devices are 32-bit elements; how exact they have to be, the bound alone decides.
A program may use at most 32 MiB of HBM per device.

```python
import jax
import jax.numpy as jnp
from jax import lax

NODE = 512
FACE = 64
CELL_DEV = 1
LOCAL = 512
NORB = 512
DEGREE = 7
PASSES = 1
STEPS = 1
NS_ITERS = 3
CHAIN = 128
CELLS = 128
NODES_ALL = 65536


def permuted(subkey):
    return jax.random.permutation(subkey, LOCAL)


def geometry(key):
    base_key = jax.random.fold_in(key, 4041)
    chain_keys = jax.random.split(base_key, CHAIN)
    return jax.vmap(permuted)(chain_keys).astype(jnp.int32)


def draw_cell_map(key, part):
    numbering = geometry(key)
    standard = jnp.arange(CELL_DEV)[:, None] * (NODE - FACE) + jnp.arange(NODE)[None, :]
    mapped = numbering[:, standard]
    return mapped.reshape(CHAIN * CELL_DEV, NODE).astype(jnp.int32)


def draw_face_low(key, part):
    numbering = geometry(key)
    return numbering[:, :FACE].astype(jnp.int32)


def draw_face_high(key, part):
    numbering = geometry(key)
    return numbering[:, LOCAL - FACE:].astype(jnp.int32)


def draw_initial(key, part):
    base_key, row_key, column_key = jax.random.split(jax.random.fold_in(key, 77), 3)
    entries = jax.random.truncated_normal(base_key, -5.0, 5.0, (NORB, NODES_ALL), jnp.float32)
    row_scale = jnp.exp(jax.random.uniform(row_key, (NORB, 1), jnp.float32) * jnp.log(10.0))
    column_scale = jnp.exp(jax.random.uniform(column_key, (1, NODES_ALL), jnp.float32) * jnp.log(3.0))
    device_place = (jnp.arange(NODES_ALL) // LOCAL).astype(jnp.float32)
    ramp = jnp.exp(jnp.log(3.0) * device_place / (CHAIN - 1))[None, :]
    return (entries * row_scale * column_scale * ramp).astype(jnp.float32)


def draw_cell_matrices(key, part):
    base_key = jax.random.fold_in(key, 91)
    entries = jax.random.truncated_normal(base_key, -5.0, 5.0, (CELLS, NODE, NODE), jnp.float32)
    symmetric = (entries + jnp.swapaxes(entries, 1, 2)) / (2.0 * jnp.sqrt(float(NODE)))
    return symmetric.astype(jnp.float32)


def setup_inputs(seed: int = 0) -> dict:
    key_list = jax.random.split(jax.random.key(seed), 6)
    return {
        "initial": draw_initial(jax.random.fold_in(key_list[5], 71), 0),
        "cell_matrices": draw_cell_matrices(jax.random.fold_in(key_list[5], 71), 0),
        "cell_map": draw_cell_map(jax.random.fold_in(key_list[5], 71), 0),
        "face_low": draw_face_low(jax.random.fold_in(key_list[5], 71), 0),
        "face_high": draw_face_high(jax.random.fold_in(key_list[5], 71), 0),
    }


center_value = 0.6
half_width = 1.6
highest = lax.Precision.HIGHEST

def assemble(values, face_low, face_high):
    chain_rows = jnp.arange(CHAIN)[:, None]
    lower_rim = values[:, chain_rows, face_low]
    upper_rim = values[:, chain_rows, face_high]
    values = values.at[:, chain_rows, face_low].add(jnp.roll(upper_rim, 1, axis=1))
    return values.at[:, chain_rows, face_high].add(jnp.roll(lower_rim, -1, axis=1))

def apply_operator(values, matrices, cell_index, face_low, face_high):
    chain_rows = jnp.arange(CHAIN)[:, None, None]
    gathered = values[:, chain_rows, cell_index]
    product = jnp.einsum('odcn,dcmn->odcm', gathered, matrices, precision=highest)
    summed = jnp.zeros_like(values).at[:, chain_rows, cell_index].add(product)
    return assemble(summed, face_low, face_high)

def chebyshev(values, matrices, cell_index, face_low, face_high):
    previous = values
    current = (apply_operator(values, matrices, cell_index, face_low, face_high) - center_value * values) / half_width
    for degree_index in range(DEGREE - 1):
        image = apply_operator(current, matrices, cell_index, face_low, face_high)
        following = 2.0 * (image - center_value * current) / half_width - previous
        previous, current = (current, following)
    return current

def inverse_root(correlation):
    dscale = 1.0 / jnp.sqrt(jnp.diagonal(correlation))
    scaled = correlation * dscale[:, None] * dscale[None, :]
    bound_scale = jnp.max(lax.optimization_barrier(jnp.sum(jnp.abs(scaled), axis=1)))
    target = scaled / bound_scale
    identity = jnp.eye(NORB, dtype=correlation.dtype)
    root_factor = 0.5 * (3.0 * identity - target)
    for iteration in range(NS_ITERS - 1):
        inner_term = jnp.dot(root_factor, root_factor, precision=highest)
        inner_term = jnp.dot(target, inner_term, precision=highest)
        inner_term = jnp.dot(root_factor, inner_term, precision=highest)
        root_factor = 0.5 * (3.0 * root_factor - inner_term)
    return (dscale, bound_scale, root_factor)

def reference(initial, cell_matrices, cell_map, face_low, face_high):
    matrices = cell_matrices.reshape(CHAIN, CELL_DEV, NODE, NODE)
    cell_index = cell_map.reshape(CHAIN, CELL_DEV, NODE)
    owned = jnp.ones((CHAIN, LOCAL), jnp.float32).at[jnp.arange(CHAIN)[:, None], face_low].set(0.0)
    owned_count = CHAIN * (LOCAL - FACE)
    values = assemble(initial.reshape(NORB, CHAIN, LOCAL) * owned[None], face_low, face_high)
    for step_index in range(STEPS):
        for pass_index in range(PASSES):
            values = chebyshev(values, matrices, cell_index, face_low, face_high)
        flattened = values.reshape(NORB, CHAIN * LOCAL)
        weights = owned.reshape(1, CHAIN * LOCAL)
        correlation = jnp.dot(flattened * weights, flattened.T, precision=highest) / owned_count
        dscale, bound_scale, root_factor = inverse_root(correlation)
        mixing = dscale[:, None] * root_factor / jnp.sqrt(bound_scale)
        values = jnp.dot(mixing.T, flattened, precision=highest).reshape(NORB, CHAIN, LOCAL)
    return values.reshape(NORB, CHAIN * LOCAL)
```

```python
import jax
import jax.numpy as jnp
from jax import lax
from jax.experimental import pallas as pl
from jax.experimental.pallas import tpu as pltpu
from jax.sharding import PartitionSpec as P

DEGREE = 7
NS_ITERS = 3
NODE = 512
FACE = 64
RIM = 2 * FACE
NORB = 512
WIDTH = 64
NX, NY, NZ, NEAR = 4, 4, 32, 4
FAR = NZ // NEAR
GROUP = NY * NEAR
MESH = pl.DeviceIdType.MESH

center_value = 0.6
half_width = 1.6
f32, bf16 = jnp.float32, jnp.bfloat16


def split(a):
    hi = a.astype(bf16)
    return hi, (a - hi.astype(f32)).astype(bf16)


def dot(a, b):
    return jnp.dot(a, b, preferred_element_type=f32)


def dot_t(a, b):
    return lax.dot_general(a, b, (((1,), (1,)), ((), ())), preferred_element_type=f32)


def product(a, b_hi, b_lo, mul=dot):
    hi, lo = split(a)
    rows = a.shape[0]
    both = mul(jnp.concatenate([hi, lo], axis=0), b_hi)
    return both[:rows] + (both[rows:] + mul(hi, b_lo))


def rows_of(ref, start, count):
    return ref.at[pl.ds(pl.multiple_of(start, count), count), :]


def ring_gather(buf, c, x, k, ssem, rsem):
    me = 2 * x + k
    right = 2 * lax.rem(x + 1, NX) + k
    left = 2 * lax.rem(x + NX - 1, NX) + k
    across = 2 * lax.rem(x + 2, NX) + k
    other = 2 * x + (1 - k)

    def send(block, half, slot, target):
        if half is None:
            ref = rows_of(buf, block * WIDTH, WIDTH)
        else:
            ref = rows_of(buf, block * WIDTH + half * (WIDTH // 2), WIDTH // 2)
        copy = pltpu.make_async_remote_copy(
            src_ref=ref, dst_ref=ref, send_sem=ssem.at[slot], recv_sem=rsem.at[slot],
            device_id=(c, target), device_id_type=MESH,
        )
        copy.start()
        return copy

    r0 = send(me, 0, 0, right)
    l1 = send(me, 1, 1, left)
    r1 = send(me, 1, 2, right)
    l0 = send(me, 0, 3, left)
    own = send(me, None, 4, other)
    r0.wait_recv()
    on = send(left, 0, 5, right)
    l1.wait_recv()
    back = send(right, 1, 6, left)
    r1.wait_recv()
    p_left = send(left, None, 7, other)
    l0.wait_recv()
    p_right = send(right, None, 8, other)
    on.wait_recv()
    back.wait_recv()
    p_across = send(across, None, 9, other)
    for copy in (own, p_left, p_right, p_across):
        copy.wait_recv()
    for copy in (r0, l1, r1, l0, own, on, back, p_left, p_right, p_across):
        copy.wait_send()


def kernel(
    initial, matrices, cmap_ref, low_ref, high_ref, out_ref,
    init_v, mat_v, q_ref, ah, al, cur, prev, sbuf, rbuf,
    xbuf, nh, nl, cpart, rsbuf, zbuf, corr, th, tl, root, rh, rl,
    load_sem, hs, hr, xs, xr, rs_s, rs_r, z_s, z_r, g_s, g_r, cs, cr,
):
    c = lax.axis_index("cells")
    o = lax.axis_index("orb")
    cells = NY * NZ
    x, k = o // 2, lax.rem(o, 2)
    y, z = c // NZ, lax.rem(c, NZ)
    far, near = z // NEAR, lax.rem(z, NEAR)
    g = y * NEAR + near
    after = lax.rem(c + 1, cells)
    before = lax.rem(c + cells - 1, cells)

    def member(p):
        return (p // NEAR) * NZ + far * NEAR + lax.rem(p, NEAR)

    def distant(q):
        return y * NZ + q * NEAR + near

    load_a = pltpu.make_async_copy(matrices.at[0], mat_v, load_sem.at[0])
    load_x = pltpu.make_async_copy(initial, init_v, load_sem.at[1])
    load_a.start()
    load_x.start()

    barrier = pltpu.get_barrier_semaphore()
    peers = [(distant(lax.rem(far + d, FAR)), o) for d in (4, 3, 5, 2, 6, 1, 7)]
    peers += [(member(lax.rem(g + d, GROUP)), o) for d in range(1, GROUP)]
    peers += [(after, o), (before, o)]
    peers += [
        (c, 2 * lax.rem(x + 1, NX) + k),
        (c, 2 * lax.rem(x + NX - 1, NX) + k),
        (c, 2 * x + (1 - k)),
    ]
    for peer in peers:
        pl.semaphore_signal(barrier, inc=1, device_id=peer, device_id_type=MESH)

    square = (NODE, NODE)
    down = lax.broadcasted_iota(jnp.int32, square, 0).astype(f32)
    along = lax.broadcasted_iota(jnp.int32, square, 1).astype(f32)
    eye64 = lax.broadcasted_iota(jnp.int32, (FACE, FACE), 0) == lax.broadcasted_iota(
        jnp.int32, (FACE, FACE), 1
    )

    def one_hot(mask):
        return jnp.where(mask, 1.0, 0.0).astype(bf16)

    def upright(ref):
        wide = jnp.broadcast_to(ref[...].astype(f32), (FACE, FACE))
        return jnp.sum(jnp.where(eye64, wide, 0.0), axis=1, keepdims=True)

    lanes = lax.broadcasted_iota(jnp.int32, (FACE, NODE), 1).astype(f32)
    ranks = lax.broadcasted_iota(jnp.int32, (FACE, NODE), 0).astype(f32)
    is_low = jnp.where(upright(low_ref) == lanes, 1.0, 0.0)
    is_high = jnp.where(upright(high_ref) == lanes, 1.0, 0.0)
    is_face = jnp.sum(is_low + is_high, axis=0, keepdims=True)
    face_place = jnp.sum(is_low * ranks + is_high * (ranks + FACE), axis=0, keepdims=True)
    others = jnp.broadcast_to(1.0 - is_face, (16, NODE)).astype(bf16)
    rank = dot(others, one_hot(down < along))[0:1]
    place = jnp.where(is_face > 0.5, face_place, rank + RIM)
    cmap = cmap_ref[...].astype(f32)
    at_cell = one_hot(down == cmap)
    upper = jnp.where(place >= 256.0, 1.0, 0.0)
    parts = lax.broadcasted_iota(jnp.int32, (16, NODE), 0)
    coded = jnp.where(
        parts == 0,
        jnp.broadcast_to(upper, (16, NODE)),
        jnp.broadcast_to(place - 256.0 * upper, (16, NODE)),
    ).astype(bf16)
    moved = dot(coded, at_cell)
    cell_place = moved[0:1] * 256.0 + moved[1:2]
    q_ref[...] = one_hot(down == place)
    by_cell = one_hot(down == cell_place)
    load_a.wait()
    a_hi, a_lo = split(mat_v[...])
    ah[...] = dot_t(dot(by_cell, a_hi).astype(bf16), by_cell).astype(bf16)
    al[...] = dot_t(dot(by_cell, a_lo).astype(bf16), by_cell).astype(bf16)
    load_x.wait()
    x_hi, x_lo = split(init_v[...])
    x_rest = (init_v[...] - x_hi.astype(f32) - x_lo.astype(f32)).astype(bf16)
    stacked = dot_t(jnp.concatenate([x_hi, x_lo, x_rest], axis=0), q_ref[...])
    cur[...] = stacked[0:64] + (stacked[64:128] + stacked[128:192])
    prev[...] = jnp.zeros_like(prev)

    half = WIDTH // 2
    left_lanes = lax.broadcasted_iota(jnp.int32, (half, RIM), 1) < FACE

    def to_before(rim):
        return jnp.where(left_lanes, rim[:half], pltpu.roll(rim[half:], FACE, 1))

    def to_after(rim):
        return jnp.where(left_lanes, pltpu.roll(rim[:half], FACE, 1), rim[half:])

    def halo_copy(slot, way):
        return pltpu.make_async_remote_copy(
            src_ref=sbuf.at[slot, way], dst_ref=rbuf.at[slot, way],
            send_sem=hs.at[slot, way], recv_sem=hr.at[slot, way],
            device_id=(after if way == 1 else before, o), device_id_type=MESH,
        )

    sbuf[0, 1] = to_after(cur[:, :RIM])
    pl.semaphore_wait(barrier, len(peers))
    start = halo_copy(0, 1)
    start.start()
    start.wait()
    got = rbuf[0, 1]
    first_rim = cur[:, :RIM]
    cur[:half, :RIM] = jnp.where(left_lanes, got, first_rim[:half])
    cur[half:, :RIM] = jnp.where(left_lanes, pltpu.roll(got, FACE, 1), first_rim[half:])

    def step(index, carry):
        slot = index + 1
        now = cur[...]
        hi, lo = split(now)
        both = jnp.concatenate([hi, lo], axis=0)

        def apply(begin, end):
            main = dot(both, ah[:, begin:end])
            return main[:WIDTH] + (main[WIDTH:] + dot(hi, al[:, begin:end]))

        rim = apply(0, RIM)
        sbuf[slot, 0] = to_before(rim)
        sbuf[slot, 1] = to_after(rim)
        down_copy = halo_copy(slot, 0)
        up_copy = halo_copy(slot, 1)
        down_copy.start()
        up_copy.start()
        factor = jnp.where(index == 0, 1.0, 2.0)
        inner = apply(RIM, NODE)
        following = (
            factor * (inner - center_value * now[:, RIM:]) / half_width - prev[:, RIM:]
        )
        prev[:, RIM:] = now[:, RIM:]
        cur[:, RIM:] = following
        down_copy.wait()
        up_copy.wait()
        from_next = rbuf[slot, 0]
        from_last = rbuf[slot, 1]
        add_top = jnp.where(left_lanes, from_last, pltpu.roll(from_next, FACE, 1))
        add_bottom = jnp.where(left_lanes, pltpu.roll(from_last, FACE, 1), from_next)
        image = rim + jnp.concatenate([add_top, add_bottom], axis=0)
        edge = factor * (image - center_value * now[:, :RIM]) / half_width - prev[:, :RIM]
        prev[:, :RIM] = now[:, :RIM]
        cur[:, :RIM] = edge
        return carry

    lax.fori_loop(0, DEGREE, step, 0)

    xbuf[pl.ds(pl.multiple_of(o * WIDTH, WIDTH), WIDTH), :] = cur[...]
    ring_gather(xbuf, c, x, k, xs, xr)

    e_hi, e_lo = split(xbuf[...])
    owned = lax.broadcasted_iota(jnp.int32, (WIDTH, NODE), 1) >= FACE
    cpart[...] = product(jnp.where(owned, cur[...], 0.0), e_hi, e_lo, dot_t)

    def piece(p):
        return p // 8, lax.rem(p, 8)

    def slab(ref, base, p):
        side, row = piece(p)
        return ref.at[
            pl.ds(pl.multiple_of(base + row * 8, 8), 8),
            pl.ds(pl.multiple_of(side * 256, 256), 256),
        ]

    shares = []
    for d in range(1, GROUP):
        p = lax.rem(g + d, GROUP)
        copy = pltpu.make_async_remote_copy(
            src_ref=slab(cpart, 0, p), dst_ref=rsbuf.at[g],
            send_sem=rs_s.at[d], recv_sem=rs_r.at[d],
            device_id=(member(p), o), device_id_type=MESH,
        )
        copy.start()
        shares.append(copy)
    nh[...] = dot(e_hi, q_ref[...]).astype(bf16)
    nl[...] = dot(e_lo, q_ref[...]).astype(bf16)
    side, row = piece(g)
    rsbuf[g] = cpart[
        pl.ds(pl.multiple_of(row * 8, 8), 8), pl.ds(pl.multiple_of(side * 256, 256), 256)
    ]
    for copy in shares:
        copy.wait_recv()
    zbuf[far] = jnp.sum(rsbuf[...], axis=0)
    sums = []
    for d in (4, 3, 5, 2, 6, 1, 7):
        copy = pltpu.make_async_remote_copy(
            src_ref=zbuf.at[far], dst_ref=zbuf.at[far],
            send_sem=z_s.at[d], recv_sem=z_r.at[d],
            device_id=(distant(lax.rem(far + d, FAR)), o), device_id_type=MESH,
        )
        copy.start()
        sums.append(copy)
    for copy in shares:
        copy.wait_send()
    for copy in sums:
        copy.wait_recv()
    total = jnp.sum(zbuf[...], axis=0) / float(cells * (NODE - FACE))
    mine = o * WIDTH
    corr[
        pl.ds(pl.multiple_of(mine + row * 8, 8), 8), pl.ds(pl.multiple_of(side * 256, 256), 256)
    ] = total
    spread = []
    for d in range(1, GROUP):
        ref = slab(corr, mine, g)
        copy = pltpu.make_async_remote_copy(
            src_ref=ref, dst_ref=ref, send_sem=g_s.at[d], recv_sem=g_r.at[d],
            device_id=(member(lax.rem(g + d, GROUP)), o), device_id_type=MESH,
        )
        copy.start()
        spread.append(copy)
    for copy in sums:
        copy.wait_send()
    for copy in spread:
        copy.wait_recv()
    for copy in spread:
        copy.wait_send()
    ring_gather(corr, c, x, k, cs, cr)

    full = corr[...]
    diagonal = jnp.where(down == along, full, 0.0)
    d_along = 1.0 / jnp.sqrt(jnp.sum(diagonal, axis=0, keepdims=True))
    d_down = 1.0 / jnp.sqrt(jnp.sum(diagonal, axis=1, keepdims=True))
    scaled = full * d_down * d_along
    bound = jnp.max(jnp.sum(jnp.abs(scaled), axis=1, keepdims=True), axis=0, keepdims=True)
    target = scaled / bound
    hi, lo = split(target)
    th[...] = hi
    tl[...] = lo
    root[...] = 0.5 * (jnp.where(down == along, 3.0, 0.0) - target)
    for iteration in range(NS_ITERS - 2):
        hi, lo = split(root[...])
        rh[...] = hi
        rl[...] = lo
        inner = product(root[...], rh[...], rl[...])
        in_hi, in_lo = split(inner)
        inner = product(target, in_hi, in_lo)
        in_hi, in_lo = split(inner)
        inner = product(root[...], in_hi, in_lo)
        root[...] = 0.5 * (3.0 * root[...] - inner)
    hi, lo = split(root[...])
    rh[...] = hi
    rl[...] = lo
    block = root[pl.ds(pl.multiple_of(mine, WIDTH), WIDTH), :]
    inner = product(block, rh[...], rl[...])
    inner = product(inner, th[...], tl[...])
    inner = product(inner, rh[...], rl[...])
    block = 0.5 * (3.0 * block - inner)
    mixing = block * d_along / jnp.sqrt(bound)
    out_ref[...] = product(mixing, nh[...], nl[...])


def body(initial, cell_matrices, cell_map, face_low, face_high):
    vmem = pl.BlockSpec(memory_space=pltpu.VMEM)
    hbm = pl.BlockSpec(memory_space=pl.ANY)
    dma = pltpu.SemaphoreType.DMA
    half = WIDTH // 2
    return pl.pallas_call(
        kernel,
        out_shape=jax.ShapeDtypeStruct((WIDTH, NODE), f32),
        in_specs=[hbm, hbm, vmem, vmem, vmem],
        out_specs=vmem,
        scratch_shapes=[
            pltpu.VMEM((WIDTH, NODE), f32),
            pltpu.VMEM((NODE, NODE), f32),
            pltpu.VMEM((NODE, NODE), bf16),
            pltpu.VMEM((NODE, NODE), bf16),
            pltpu.VMEM((NODE, NODE), bf16),
            pltpu.VMEM((WIDTH, NODE), f32),
            pltpu.VMEM((WIDTH, NODE), f32),
            pltpu.VMEM((DEGREE + 1, 2, half, RIM), f32),
            pltpu.VMEM((DEGREE + 1, 2, half, RIM), f32),
            pltpu.VMEM((NORB, NODE), f32),
            pltpu.VMEM((NORB, NODE), bf16),
            pltpu.VMEM((NORB, NODE), bf16),
            pltpu.VMEM((WIDTH, NORB), f32),
            pltpu.VMEM((GROUP, 8, 256), f32),
            pltpu.VMEM((FAR, 8, 256), f32),
            pltpu.VMEM((NORB, NORB), f32),
            pltpu.VMEM((NORB, NORB), bf16),
            pltpu.VMEM((NORB, NORB), bf16),
            pltpu.VMEM((NORB, NORB), f32),
            pltpu.VMEM((NORB, NORB), bf16),
            pltpu.VMEM((NORB, NORB), bf16),
            dma((2,)),
            dma((DEGREE + 1, 2)), dma((DEGREE + 1, 2)),
            dma((10,)), dma((10,)),
            dma((GROUP,)), dma((GROUP,)),
            dma((FAR,)), dma((FAR,)),
            dma((GROUP,)), dma((GROUP,)),
            dma((10,)), dma((10,)),
        ],
        compiler_params=pltpu.CompilerParams(collective_id=0, has_side_effects=True),
        name="subspace_step",
    )(initial, cell_matrices, cell_map, face_low, face_high)


def solution(mesh):
    placed = (
        P("orb", "cells"),
        P("cells", None, None),
        P("cells", None),
        P("cells", None),
        P("cells", None),
    )
    return jax.shard_map(
        body, mesh=mesh, in_specs=placed, out_specs=P("orb", "cells"), check_vma=False
    )
```

```python
import jax
import jax.numpy as jnp
from jax import lax
from jax.experimental import pallas as pl
from jax.experimental.pallas import tpu as pltpu
from jax.sharding import PartitionSpec as P

DEGREE = 7
NS_ITERS = 3
NODE = 512
FACE = 64
RIM = 2 * FACE
NORB = 512
WIDTH = 64
NX, NY, NZ, NEAR = 4, 4, 32, 4
FAR = NZ // NEAR
GROUP = NY * NEAR
MESH = pl.DeviceIdType.MESH

center_value = 0.6
half_width = 1.6
f32, bf16 = jnp.float32, jnp.bfloat16


def split(a):
    hi = a.astype(bf16)
    return hi, (a - hi.astype(f32)).astype(bf16)


def dot(a, b):
    return jnp.dot(a, b, preferred_element_type=f32)


def dot_t(a, b):
    return lax.dot_general(a, b, (((1,), (1,)), ((), ())), preferred_element_type=f32)


def product(a, b_hi, b_lo, mul=dot):
    hi, lo = split(a)
    rows = a.shape[0]
    both = mul(jnp.concatenate([hi, lo], axis=0), b_hi)
    return both[:rows] + (both[rows:] + mul(hi, b_lo))


def rows_of(ref, start, count):
    return ref.at[pl.ds(pl.multiple_of(start, count), count), :]


def ring_gather(buf, c, x, k, ssem, rsem):
    me = 2 * x + k
    right = 2 * lax.rem(x + 1, NX) + k
    left = 2 * lax.rem(x + NX - 1, NX) + k
    across = 2 * lax.rem(x + 2, NX) + k
    other = 2 * x + (1 - k)

    def send(block, half, slot, target):
        if half is None:
            ref = rows_of(buf, block * WIDTH, WIDTH)
        else:
            ref = rows_of(buf, block * WIDTH + half * (WIDTH // 2), WIDTH // 2)
        copy = pltpu.make_async_remote_copy(
            src_ref=ref, dst_ref=ref, send_sem=ssem.at[slot], recv_sem=rsem.at[slot],
            device_id=(c, target), device_id_type=MESH,
        )
        copy.start()
        return copy

    r0 = send(me, 0, 0, right)
    l1 = send(me, 1, 1, left)
    r1 = send(me, 1, 2, right)
    l0 = send(me, 0, 3, left)
    own = send(me, None, 4, other)
    r0.wait_recv()
    on = send(left, 0, 5, right)
    l1.wait_recv()
    back = send(right, 1, 6, left)
    r1.wait_recv()
    p_left = send(left, None, 7, other)
    l0.wait_recv()
    p_right = send(right, None, 8, other)
    on.wait_recv()
    back.wait_recv()
    p_across = send(across, None, 9, other)
    for copy in (own, p_left, p_right, p_across):
        copy.wait_recv()
    for copy in (r0, l1, r1, l0, own, on, back, p_left, p_right, p_across):
        copy.wait_send()


def kernel(
    initial, matrices, cmap_ref, low_ref, high_ref, out_ref,
    init_v, mat_v, q_ref, ah, al, cur, prev, image, sbuf, rbuf,
    xbuf, nh, nl, cpart, rsbuf, zbuf, corr, th, tl, root, rh, rl,
    load_sem, hs, hr, xs, xr, rs_s, rs_r, z_s, z_r, g_s, g_r, cs, cr, far_sem,
):
    c = lax.axis_index("cells")
    o = lax.axis_index("orb")
    cells = NY * NZ
    x, k = o // 2, lax.rem(o, 2)
    y, z = c // NZ, lax.rem(c, NZ)
    far, near = z // NEAR, lax.rem(z, NEAR)
    g = y * NEAR + near
    after = lax.rem(c + 1, cells)
    before = lax.rem(c + cells - 1, cells)

    def member(p):
        return (p // NEAR) * NZ + far * NEAR + lax.rem(p, NEAR)

    def distant(q):
        return y * NZ + q * NEAR + near

    load_a = pltpu.make_async_copy(matrices.at[0], mat_v, load_sem.at[0])
    load_x = pltpu.make_async_copy(initial, init_v, load_sem.at[1])
    load_a.start()
    load_x.start()

    barrier = pltpu.get_barrier_semaphore()
    def ring_z(d):
        return (y * NZ + lax.rem(z + d + NZ, NZ), o)

    def ring_y(d):
        return (lax.rem(y + d + NY, NY) * NZ + z, o)

    peers = [ring_z(1), ring_z(-1), ring_y(1), ring_y(-1)]
    peers += [(after, o), (before, o)]
    peers += [
        (c, 2 * lax.rem(x + 1, NX) + k),
        (c, 2 * lax.rem(x + NX - 1, NX) + k),
        (c, 2 * x + (1 - k)),
    ]
    for peer in peers:
        pl.semaphore_signal(barrier, inc=1, device_id=peer, device_id_type=MESH)

    square = (NODE, NODE)
    down = lax.broadcasted_iota(jnp.int32, square, 0).astype(f32)
    along = lax.broadcasted_iota(jnp.int32, square, 1).astype(f32)
    eye64 = lax.broadcasted_iota(jnp.int32, (FACE, FACE), 0) == lax.broadcasted_iota(
        jnp.int32, (FACE, FACE), 1
    )

    def one_hot(mask):
        return jnp.where(mask, 1.0, 0.0).astype(bf16)

    def upright(ref):
        wide = jnp.broadcast_to(ref[...].astype(f32), (FACE, FACE))
        return jnp.sum(jnp.where(eye64, wide, 0.0), axis=1, keepdims=True)

    lanes = lax.broadcasted_iota(jnp.int32, (FACE, NODE), 1).astype(f32)
    ranks = lax.broadcasted_iota(jnp.int32, (FACE, NODE), 0).astype(f32)
    is_low = jnp.where(upright(low_ref) == lanes, 1.0, 0.0)
    is_high = jnp.where(upright(high_ref) == lanes, 1.0, 0.0)
    is_face = jnp.sum(is_low + is_high, axis=0, keepdims=True)
    face_place = jnp.sum(is_low * ranks + is_high * (ranks + FACE), axis=0, keepdims=True)
    others = jnp.broadcast_to(1.0 - is_face, (16, NODE)).astype(bf16)
    rank = dot(others, one_hot(down < along))[0:1]
    place = jnp.where(is_face > 0.5, face_place, rank + RIM)
    q_ref[...] = one_hot(down == place)
    load_x.wait()
    x_hi, x_lo = split(init_v[...])
    x_rest = (init_v[...] - x_hi.astype(f32) - x_lo.astype(f32)).astype(bf16)
    stacked = dot_t(jnp.concatenate([x_hi, x_lo, x_rest], axis=0), q_ref[...])
    cur[...] = stacked[0:64] + (stacked[64:128] + stacked[128:192])
    prev[...] = jnp.zeros_like(prev)

    half = WIDTH // 2
    left_lanes = lax.broadcasted_iota(jnp.int32, (half, RIM), 1) < FACE

    def to_before(rim):
        return jnp.where(left_lanes, rim[:half], pltpu.roll(rim[half:], FACE, 1))

    def to_after(rim):
        return jnp.where(left_lanes, pltpu.roll(rim[:half], FACE, 1), rim[half:])

    def halo_copy(slot, way):
        return pltpu.make_async_remote_copy(
            src_ref=sbuf.at[slot, way], dst_ref=rbuf.at[slot, way],
            send_sem=hs.at[slot, way], recv_sem=hr.at[slot, way],
            device_id=(after if way == 1 else before, o), device_id_type=MESH,
        )

    sbuf[0, 1] = to_after(cur[:, :RIM])
    pl.semaphore_wait(barrier, len(peers))
    start = halo_copy(0, 1)
    start.start()
    stages = [ring_z(1), ring_z(-1)], [ring_z(2), ring_z(-2)], [ring_z(4), ring_z(-4)]
    stages += ([ring_z(8), ring_z(-8)], [ring_y(1), ring_y(-1)], [ring_y(1), ring_y(-1)])

    def greet(stage):
        for peer in stages[stage]:
            pl.semaphore_signal(far_sem.at[stage], inc=1, device_id=peer, device_id_type=MESH)

    def greeted(stage):
        pl.semaphore_wait(far_sem.at[stage], 2)

    greet(0)
    cmap = cmap_ref[...].astype(f32)
    at_cell = one_hot(down == cmap)
    upper = jnp.where(place >= 256.0, 1.0, 0.0)
    parts = lax.broadcasted_iota(jnp.int32, (16, NODE), 0)
    coded = jnp.where(
        parts == 0,
        jnp.broadcast_to(upper, (16, NODE)),
        jnp.broadcast_to(place - 256.0 * upper, (16, NODE)),
    ).astype(bf16)
    moved = dot(coded, at_cell)
    cell_place = moved[0:1] * 256.0 + moved[1:2]
    by_cell = one_hot(down == cell_place)
    load_a.wait()
    a_hi, a_lo = split(mat_v[...])
    ah[...] = dot_t(dot(by_cell, a_hi).astype(bf16), by_cell).astype(bf16)
    al[...] = dot_t(dot(by_cell, a_lo).astype(bf16), by_cell).astype(bf16)

    def apply(a, begin, end, first, last):
        hi, lo = split(a)
        rows = slice(begin, end)
        main = dot(jnp.concatenate([hi, lo], axis=0), ah[rows, first:last])
        return main[:WIDTH] + (main[WIDTH:] + dot(hi, al[rows, first:last]))

    def ahead():
        image[...] = apply(cur[:, RIM:], RIM, NODE, 0, NODE)

    ahead()
    start.wait()
    got = rbuf[0, 1]
    first_rim = cur[:, :RIM]
    cur[:half, :RIM] = jnp.where(left_lanes, got, first_rim[:half])
    cur[half:, :RIM] = jnp.where(left_lanes, pltpu.roll(got, FACE, 1), first_rim[half:])

    def step(index, carry):
        slot = index + 1
        now = cur[:, :RIM]
        rim = image[:, :RIM] + apply(now, 0, RIM, 0, RIM)
        sbuf[slot, 0] = to_before(rim)
        sbuf[slot, 1] = to_after(rim)
        down_copy = halo_copy(slot, 0)
        up_copy = halo_copy(slot, 1)
        down_copy.start()
        up_copy.start()
        for stage, when in enumerate((0, 1, 2, 4, 5)):
            @pl.when(index == when)
            def _():
                greeted(stage)
                greet(stage + 1)
        factor = jnp.where(index == 0, 1.0, 2.0)
        inner = image[:, RIM:] + apply(now, 0, RIM, RIM, NODE)
        core = cur[:, RIM:]
        following = factor * (inner - center_value * core) / half_width - prev[:, RIM:]
        prev[:, RIM:] = core
        cur[:, RIM:] = following
        ahead()
        down_copy.wait()
        up_copy.wait()
        from_next = rbuf[slot, 0]
        from_last = rbuf[slot, 1]
        add_top = jnp.where(left_lanes, from_last, pltpu.roll(from_next, FACE, 1))
        add_bottom = jnp.where(left_lanes, pltpu.roll(from_last, FACE, 1), from_next)
        rim = rim + jnp.concatenate([add_top, add_bottom], axis=0)
        edge = factor * (rim - center_value * now) / half_width - prev[:, :RIM]
        prev[:, :RIM] = now
        cur[:, :RIM] = edge
        return carry

    lax.fori_loop(0, DEGREE, step, 0)

    xbuf[pl.ds(pl.multiple_of(o * WIDTH, WIDTH), WIDTH), :] = cur[...]
    ring_gather(xbuf, c, x, k, xs, xr)
    greeted(5)

    e_hi, e_lo = split(xbuf[...])
    owned = lax.broadcasted_iota(jnp.int32, (WIDTH, NODE), 1) >= FACE
    cpart[...] = product(jnp.where(owned, cur[...], 0.0), e_hi, e_lo, dot_t)

    def piece(p):
        return p // 8, lax.rem(p, 8)

    def slab(ref, base, p):
        side, row = piece(p)
        return ref.at[
            pl.ds(pl.multiple_of(base + row * 8, 8), 8),
            pl.ds(pl.multiple_of(side * 256, 256), 256),
        ]

    shares = []
    for d in range(1, GROUP):
        p = lax.rem(g + d, GROUP)
        copy = pltpu.make_async_remote_copy(
            src_ref=slab(cpart, 0, p), dst_ref=rsbuf.at[g],
            send_sem=rs_s.at[d], recv_sem=rs_r.at[d],
            device_id=(member(p), o), device_id_type=MESH,
        )
        copy.start()
        shares.append(copy)
    nh[...] = dot(e_hi, q_ref[...]).astype(bf16)
    nl[...] = dot(e_lo, q_ref[...]).astype(bf16)
    side, row = piece(g)
    rsbuf[g] = cpart[
        pl.ds(pl.multiple_of(row * 8, 8), 8), pl.ds(pl.multiple_of(side * 256, 256), 256)
    ]
    for copy in shares:
        copy.wait_recv()
    zbuf[far] = jnp.sum(rsbuf[...], axis=0)
    sums = []
    for d in (4, 3, 5, 2, 6, 1, 7):
        copy = pltpu.make_async_remote_copy(
            src_ref=zbuf.at[far], dst_ref=zbuf.at[far],
            send_sem=z_s.at[d], recv_sem=z_r.at[d],
            device_id=(distant(lax.rem(far + d, FAR)), o), device_id_type=MESH,
        )
        copy.start()
        sums.append(copy)
    for copy in shares:
        copy.wait_send()
    for copy in sums:
        copy.wait_recv()
    total = jnp.sum(zbuf[...], axis=0) / float(cells * (NODE - FACE))
    mine = o * WIDTH
    corr[
        pl.ds(pl.multiple_of(mine + row * 8, 8), 8), pl.ds(pl.multiple_of(side * 256, 256), 256)
    ] = total
    spread = []
    for d in range(1, GROUP):
        ref = slab(corr, mine, g)
        copy = pltpu.make_async_remote_copy(
            src_ref=ref, dst_ref=ref, send_sem=g_s.at[d], recv_sem=g_r.at[d],
            device_id=(member(lax.rem(g + d, GROUP)), o), device_id_type=MESH,
        )
        copy.start()
        spread.append(copy)
    for copy in sums:
        copy.wait_send()
    for copy in spread:
        copy.wait_recv()
    for copy in spread:
        copy.wait_send()
    ring_gather(corr, c, x, k, cs, cr)

    full = corr[...]
    diagonal = jnp.where(down == along, full, 0.0)
    d_along = 1.0 / jnp.sqrt(jnp.sum(diagonal, axis=0, keepdims=True))
    d_down = 1.0 / jnp.sqrt(jnp.sum(diagonal, axis=1, keepdims=True))
    scaled = full * d_down * d_along
    bound = jnp.max(jnp.sum(jnp.abs(scaled), axis=1, keepdims=True), axis=0, keepdims=True)
    target = scaled / bound
    hi, lo = split(target)
    th[...] = hi
    tl[...] = lo
    root[...] = 0.5 * (jnp.where(down == along, 3.0, 0.0) - target)
    for iteration in range(NS_ITERS - 2):
        hi, lo = split(root[...])
        rh[...] = hi
        rl[...] = lo
        inner = product(root[...], rh[...], rl[...])
        in_hi, in_lo = split(inner)
        inner = product(target, in_hi, in_lo)
        in_hi, in_lo = split(inner)
        inner = product(root[...], in_hi, in_lo)
        root[...] = 0.5 * (3.0 * root[...] - inner)
    hi, lo = split(root[...])
    rh[...] = hi
    rl[...] = lo
    block = root[pl.ds(pl.multiple_of(mine, WIDTH), WIDTH), :]
    inner = product(block, rh[...], rl[...])
    inner = product(inner, th[...], tl[...])
    inner = product(inner, rh[...], rl[...])
    block = 0.5 * (3.0 * block - inner)
    mixing = block * d_along / jnp.sqrt(bound)
    out_ref[...] = product(mixing, nh[...], nl[...])


def body(initial, cell_matrices, cell_map, face_low, face_high):
    vmem = pl.BlockSpec(memory_space=pltpu.VMEM)
    hbm = pl.BlockSpec(memory_space=pl.ANY)
    dma = pltpu.SemaphoreType.DMA
    half = WIDTH // 2
    return pl.pallas_call(
        kernel,
        out_shape=jax.ShapeDtypeStruct((WIDTH, NODE), f32),
        in_specs=[hbm, hbm, vmem, vmem, vmem],
        out_specs=vmem,
        scratch_shapes=[
            pltpu.VMEM((WIDTH, NODE), f32),
            pltpu.VMEM((NODE, NODE), f32),
            pltpu.VMEM((NODE, NODE), bf16),
            pltpu.VMEM((NODE, NODE), bf16),
            pltpu.VMEM((NODE, NODE), bf16),
            pltpu.VMEM((WIDTH, NODE), f32),
            pltpu.VMEM((WIDTH, NODE), f32),
            pltpu.VMEM((WIDTH, NODE), f32),
            pltpu.VMEM((DEGREE + 1, 2, half, RIM), f32),
            pltpu.VMEM((DEGREE + 1, 2, half, RIM), f32),
            pltpu.VMEM((NORB, NODE), f32),
            pltpu.VMEM((NORB, NODE), bf16),
            pltpu.VMEM((NORB, NODE), bf16),
            pltpu.VMEM((WIDTH, NORB), f32),
            pltpu.VMEM((GROUP, 8, 256), f32),
            pltpu.VMEM((FAR, 8, 256), f32),
            pltpu.VMEM((NORB, NORB), f32),
            pltpu.VMEM((NORB, NORB), bf16),
            pltpu.VMEM((NORB, NORB), bf16),
            pltpu.VMEM((NORB, NORB), f32),
            pltpu.VMEM((NORB, NORB), bf16),
            pltpu.VMEM((NORB, NORB), bf16),
            dma((2,)),
            dma((DEGREE + 1, 2)), dma((DEGREE + 1, 2)),
            dma((10,)), dma((10,)),
            dma((GROUP,)), dma((GROUP,)),
            dma((FAR,)), dma((FAR,)),
            dma((GROUP,)), dma((GROUP,)),
            dma((10,)), dma((10,)),
            pltpu.SemaphoreType.REGULAR((6,)),
        ],
        compiler_params=pltpu.CompilerParams(collective_id=0, has_side_effects=True),
        name="subspace_step",
    )(initial, cell_matrices, cell_map, face_low, face_high)


def solution(mesh):
    placed = (
        P("orb", "cells"),
        P("cells", None, None),
        P("cells", None),
        P("cells", None),
        P("cells", None),
    )
    return jax.shard_map(
        body, mesh=mesh, in_specs=placed, out_specs=P("orb", "cells"), check_vma=False
    )
```

```python
import jax
import jax.numpy as jnp
from jax import lax
from jax.experimental import pallas as pl
from jax.experimental.pallas import tpu as pltpu
from jax.sharding import PartitionSpec as P

DEGREE = 7
NS_ITERS = 3
NODE = 512
FACE = 64
RIM = 2 * FACE
NORB = 512
WIDTH = 64
NX, NY, NZ, NEAR = 4, 4, 32, 4
FAR = NZ // NEAR
GROUP = NY * NEAR
MESH = pl.DeviceIdType.MESH

center_value = 0.6
half_width = 1.6
f32, bf16 = jnp.float32, jnp.bfloat16


def split(a):
    hi = a.astype(bf16)
    return hi, (a - hi.astype(f32)).astype(bf16)


def dot(a, b):
    return jnp.dot(a, b, preferred_element_type=f32)


def dot_t(a, b):
    return lax.dot_general(a, b, (((1,), (1,)), ((), ())), preferred_element_type=f32)


def product(a, b_hi, b_lo, mul=dot):
    hi, lo = split(a)
    rows = a.shape[0]
    both = mul(jnp.concatenate([hi, lo], axis=0), b_hi)
    return both[:rows] + (both[rows:] + mul(hi, b_lo))


def ring_gather(view, c, x, k, ssem, rsem, first, second, passing):
    right_x, left_x = lax.rem(x + 1, NX), lax.rem(x + NX - 1, NX)
    across = lax.rem(x + 2, NX)
    right, left, other = 2 * right_x + k, 2 * left_x + k, 2 * x + (1 - k)

    def send(block, half, slot, target):
        ref = view(block, half)
        copy = pltpu.make_async_remote_copy(
            src_ref=ref, dst_ref=ref, send_sem=ssem.at[slot], recv_sem=rsem.at[slot],
            device_id=(c, target), device_id_type=MESH,
        )
        copy.start()
        return copy

    passed = []

    def pass_over(block, half):
        if half in passing:
            passed.append(send(block, (first, second)[half], 6 + len(passed), other))

    r0 = send(x, first, 0, right)
    l1 = send(x, second, 1, left)
    pass_over(x, 0)
    pass_over(x, 1)
    r1 = send(x, second, 2, right)
    l0 = send(x, first, 3, left)
    r0.wait_recv()
    on = send(left_x, first, 4, right)
    pass_over(left_x, 0)
    l1.wait_recv()
    back = send(right_x, second, 5, left)
    pass_over(right_x, 1)
    r1.wait_recv()
    pass_over(left_x, 1)
    l0.wait_recv()
    pass_over(right_x, 0)
    on.wait_recv()
    pass_over(across, 0)
    back.wait_recv()
    pass_over(across, 1)
    return [r0, l1, r1, l0, on, back], passed


def kernel(
    initial, matrices, cmap_ref, low_ref, high_ref, out_ref,
    init_v, mat_v, q_ref, ah, al, cur, prev, image, sbuf, rbuf,
    xbuf, nh, nl, cpart, rsbuf, zbuf, corr, th, tl, root, rh, rl,
    load_sem, hs, hr, xs, xr, rs_s, rs_r, z_s, z_r, g_s, g_r, cs, cr, far_sem,
):
    c = lax.axis_index("cells")
    o = lax.axis_index("orb")
    cells = NY * NZ
    x, k = o // 2, lax.rem(o, 2)
    y, z = c // NZ, lax.rem(c, NZ)
    far, near = z // NEAR, lax.rem(z, NEAR)
    g = y * NEAR + near
    after = lax.rem(c + 1, cells)
    before = lax.rem(c + cells - 1, cells)

    def member(p):
        return (p // NEAR) * NZ + far * NEAR + lax.rem(p, NEAR)

    def distant(q):
        return y * NZ + q * NEAR + near

    load_a = pltpu.make_async_copy(matrices.at[0], mat_v, load_sem.at[0])
    load_x = pltpu.make_async_copy(initial, init_v, load_sem.at[1])
    load_a.start()
    load_x.start()

    barrier = pltpu.get_barrier_semaphore()
    def ring_z(d):
        return (y * NZ + lax.rem(z + d + NZ, NZ), o)

    def ring_y(d):
        return (lax.rem(y + d + NY, NY) * NZ + z, o)

    peers = [ring_z(1), ring_z(-1), ring_y(1), ring_y(-1)]
    peers += [(after, o), (before, o)]
    peers += [
        (c, 2 * lax.rem(x + 1, NX) + k),
        (c, 2 * lax.rem(x + NX - 1, NX) + k),
        (c, 2 * x + (1 - k)),
    ]
    for peer in peers:
        pl.semaphore_signal(barrier, inc=1, device_id=peer, device_id_type=MESH)

    square = (NODE, NODE)
    down = lax.broadcasted_iota(jnp.int32, square, 0).astype(f32)
    along = lax.broadcasted_iota(jnp.int32, square, 1).astype(f32)
    eye64 = lax.broadcasted_iota(jnp.int32, (FACE, FACE), 0) == lax.broadcasted_iota(
        jnp.int32, (FACE, FACE), 1
    )

    def one_hot(mask):
        return jnp.where(mask, 1.0, 0.0).astype(bf16)

    def upright(ref):
        wide = jnp.broadcast_to(ref[...].astype(f32), (FACE, FACE))
        return jnp.sum(jnp.where(eye64, wide, 0.0), axis=1, keepdims=True)

    lanes = lax.broadcasted_iota(jnp.int32, (FACE, NODE), 1).astype(f32)
    ranks = lax.broadcasted_iota(jnp.int32, (FACE, NODE), 0).astype(f32)
    is_low = jnp.where(upright(low_ref) == lanes, 1.0, 0.0)
    is_high = jnp.where(upright(high_ref) == lanes, 1.0, 0.0)
    is_face = jnp.sum(is_low + is_high, axis=0, keepdims=True)
    face_place = jnp.sum(is_low * ranks + is_high * (ranks + FACE), axis=0, keepdims=True)
    others = jnp.broadcast_to(1.0 - is_face, (16, NODE)).astype(bf16)
    rank = dot(others, one_hot(down < along))[0:1]
    place = jnp.where(is_face > 0.5, face_place, rank + RIM)
    q_ref[...] = one_hot(down == place)
    load_x.wait()
    x_hi, x_lo = split(init_v[...])
    x_rest = (init_v[...] - x_hi.astype(f32) - x_lo.astype(f32)).astype(bf16)
    stacked = dot_t(jnp.concatenate([x_hi, x_lo, x_rest], axis=0), q_ref[...])
    cur[...] = stacked[0:64] + (stacked[64:128] + stacked[128:192])
    prev[...] = jnp.zeros_like(prev)

    half = WIDTH // 2
    left_lanes = lax.broadcasted_iota(jnp.int32, (half, RIM), 1) < FACE

    def to_before(rim):
        return jnp.where(left_lanes, rim[:half], pltpu.roll(rim[half:], FACE, 1))

    def to_after(rim):
        return jnp.where(left_lanes, pltpu.roll(rim[:half], FACE, 1), rim[half:])

    def halo_copy(slot, way):
        return pltpu.make_async_remote_copy(
            src_ref=sbuf.at[slot, way], dst_ref=rbuf.at[slot, way],
            send_sem=hs.at[slot, way], recv_sem=hr.at[slot, way],
            device_id=(after if way == 1 else before, o), device_id_type=MESH,
        )

    sbuf[0, 1] = to_after(cur[:, :RIM])
    pl.semaphore_wait(barrier, len(peers))
    start = halo_copy(0, 1)
    start.start()
    stages = [ring_z(1), ring_z(-1)], [ring_z(2), ring_z(-2)], [ring_z(4), ring_z(-4)]
    stages += ([ring_z(8), ring_z(-8)], [ring_y(1), ring_y(-1)], [ring_y(1), ring_y(-1)])

    def greet(stage):
        for peer in stages[stage]:
            pl.semaphore_signal(far_sem.at[stage], inc=1, device_id=peer, device_id_type=MESH)

    def greeted(stage):
        pl.semaphore_wait(far_sem.at[stage], 2)

    greet(0)
    cmap = cmap_ref[...].astype(f32)
    at_cell = one_hot(down == cmap)
    upper = jnp.where(place >= 256.0, 1.0, 0.0)
    parts = lax.broadcasted_iota(jnp.int32, (16, NODE), 0)
    coded = jnp.where(
        parts == 0,
        jnp.broadcast_to(upper, (16, NODE)),
        jnp.broadcast_to(place - 256.0 * upper, (16, NODE)),
    ).astype(bf16)
    moved = dot(coded, at_cell)
    cell_place = moved[0:1] * 256.0 + moved[1:2]
    by_cell = one_hot(down == cell_place)
    load_a.wait()
    a_hi, a_lo = split(mat_v[...])
    ah[...] = dot_t(dot(by_cell, a_hi).astype(bf16), by_cell).astype(bf16)
    al[...] = dot_t(dot(by_cell, a_lo).astype(bf16), by_cell).astype(bf16)

    def apply(a, begin, end, first, last):
        hi, lo = split(a)
        rows = slice(begin, end)
        main = dot(jnp.concatenate([hi, lo], axis=0), ah[rows, first:last])
        return main[:WIDTH] + (main[WIDTH:] + dot(hi, al[rows, first:last]))

    def ahead():
        image[...] = apply(cur[:, RIM:], RIM, NODE, 0, NODE)

    ahead()
    start.wait()
    got = rbuf[0, 1]
    first_rim = cur[:, :RIM]
    cur[:half, :RIM] = jnp.where(left_lanes, got, first_rim[:half])
    cur[half:, :RIM] = jnp.where(left_lanes, pltpu.roll(got, FACE, 1), first_rim[half:])

    def step(index, carry):
        slot = index + 1
        now = cur[:, :RIM]
        rim = image[:, :RIM] + apply(now, 0, RIM, 0, RIM)
        sbuf[slot, 0] = to_before(rim)
        sbuf[slot, 1] = to_after(rim)
        down_copy = halo_copy(slot, 0)
        up_copy = halo_copy(slot, 1)
        down_copy.start()
        up_copy.start()
        for stage, when in enumerate((0, 1, 2, 4, 5)):
            @pl.when(index == when)
            def _():
                greeted(stage)
                greet(stage + 1)
        factor = jnp.where(index == 0, 1.0, 2.0)
        inner = image[:, RIM:] + apply(now, 0, RIM, RIM, NODE)
        core = cur[:, RIM:]
        following = factor * (inner - center_value * core) / half_width - prev[:, RIM:]
        prev[:, RIM:] = core
        cur[:, RIM:] = following
        ahead()
        down_copy.wait()
        up_copy.wait()
        from_next = rbuf[slot, 0]
        from_last = rbuf[slot, 1]
        add_top = jnp.where(left_lanes, from_last, pltpu.roll(from_next, FACE, 1))
        add_bottom = jnp.where(left_lanes, pltpu.roll(from_last, FACE, 1), from_next)
        rim = rim + jnp.concatenate([add_top, add_bottom], axis=0)
        edge = factor * (rim - center_value * now) / half_width - prev[:, :RIM]
        prev[:, :RIM] = now
        cur[:, :RIM] = edge
        return carry

    lax.fori_loop(0, DEGREE, step, 0)

    mine = (k * NX + x) * WIDTH

    def orbitals(block, part):
        start = (k * NX + block) * WIDTH + part * half
        return xbuf.at[pl.ds(pl.multiple_of(start, half), half), :]

    xbuf[pl.ds(pl.multiple_of(mine, WIDTH), WIDTH), :] = cur[...]
    x_sent, x_passed = ring_gather(orbitals, c, x, k, xs, xr, 0, 1, (0, 1))
    greeted(5)
    for copy in x_passed[:2]:
        copy.wait_recv()

    side = pl.ds(pl.multiple_of(k * 256, 256), 256)
    e_hi, e_lo = split(xbuf[side, :])
    owned = lax.broadcasted_iota(jnp.int32, (2 * WIDTH, NODE), 1) >= FACE
    chip = jnp.concatenate(
        [xbuf[pl.ds(pl.multiple_of(b * 256 + x * WIDTH, WIDTH), WIDTH), :] for b in (0, 1)], axis=0
    )
    cpart[...] = product(jnp.where(owned, chip, 0.0), e_hi, e_lo, dot_t)

    def slab(p):
        row = (p // 8) * 256 + x * WIDTH + lax.rem(p, 8) * 8
        return pl.ds(pl.multiple_of(row, 8), 8)

    own_slab = pl.ds(pl.multiple_of(g * 8, 8), 8)
    shares = []
    for d in range(1, GROUP):
        p = lax.rem(g + d, GROUP)
        copy = pltpu.make_async_remote_copy(
            src_ref=cpart.at[pl.ds(pl.multiple_of(p * 8, 8), 8), :], dst_ref=rsbuf.at[g],
            send_sem=rs_s.at[d], recv_sem=rs_r.at[d],
            device_id=(member(p), o), device_id_type=MESH,
        )
        copy.start()
        shares.append(copy)
    rsbuf[g] = cpart[own_slab, :]
    for copy in shares:
        copy.wait_recv()
    zbuf[far] = jnp.sum(rsbuf[...], axis=0)
    sums = []
    for d in (4, 3, 5, 2, 6, 1, 7):
        copy = pltpu.make_async_remote_copy(
            src_ref=zbuf.at[far], dst_ref=zbuf.at[far],
            send_sem=z_s.at[d], recv_sem=z_r.at[d],
            device_id=(distant(lax.rem(far + d, FAR)), o), device_id_type=MESH,
        )
        copy.start()
        sums.append(copy)
    for copy in x_passed[2:]:
        copy.wait_recv()
    e_hi, e_lo = split(xbuf[...])
    nh[...] = dot(e_hi, q_ref[...]).astype(bf16)
    nl[...] = dot(e_lo, q_ref[...]).astype(bf16)
    for copy in shares + x_sent + x_passed:
        copy.wait_send()
    for copy in sums:
        copy.wait_recv()
    total = jnp.sum(zbuf[...], axis=0) / float(cells * (NODE - FACE))
    corr[k, slab(g)] = total
    spread = []
    for d in range(1, GROUP):
        ref = corr.at[k, slab(g)]
        copy = pltpu.make_async_remote_copy(
            src_ref=ref, dst_ref=ref, send_sem=g_s.at[d], recv_sem=g_r.at[d],
            device_id=(member(lax.rem(g + d, GROUP)), o), device_id_type=MESH,
        )
        copy.start()
        spread.append(copy)
    for copy in sums:
        copy.wait_send()
    for copy in spread:
        copy.wait_recv()
    for copy in spread:
        copy.wait_send()

    def quarter(block, part):
        return corr.at[k, pl.ds(pl.multiple_of(part * 256 + block * WIDTH, WIDTH), WIDTH)]

    c_sent, c_passed = ring_gather(quarter, c, x, k, cs, cr, k, 1 - k, (0,))
    off_side = pl.ds(pl.multiple_of((1 - k) * 256, 256), 256)
    corr[1 - k, side] = corr[k, off_side].T
    for copy in c_passed:
        copy.wait_recv()
    for copy in c_sent + c_passed:
        copy.wait_send()

    full = jnp.concatenate([corr[0], corr[1]], axis=1)
    diagonal = jnp.where(down == along, full, 0.0)
    d_along = 1.0 / jnp.sqrt(jnp.sum(diagonal, axis=0, keepdims=True))
    d_down = 1.0 / jnp.sqrt(jnp.sum(diagonal, axis=1, keepdims=True))
    scaled = full * d_down * d_along
    bound = jnp.max(jnp.sum(jnp.abs(scaled), axis=1, keepdims=True), axis=0, keepdims=True)
    target = scaled / bound
    hi, lo = split(target)
    th[...] = hi
    tl[...] = lo
    root[...] = 0.5 * (jnp.where(down == along, 3.0, 0.0) - target)
    for iteration in range(NS_ITERS - 2):
        hi, lo = split(root[...])
        rh[...] = hi
        rl[...] = lo
        inner = product(root[...], rh[...], rl[...])
        in_hi, in_lo = split(inner)
        inner = product(target, in_hi, in_lo)
        in_hi, in_lo = split(inner)
        inner = product(root[...], in_hi, in_lo)
        root[...] = 0.5 * (3.0 * root[...] - inner)
    hi, lo = split(root[...])
    rh[...] = hi
    rl[...] = lo
    block = root[pl.ds(pl.multiple_of(mine, WIDTH), WIDTH), :]
    inner = product(block, rh[...], rl[...])
    inner = product(inner, th[...], tl[...])
    inner = product(inner, rh[...], rl[...])
    block = 0.5 * (3.0 * block - inner)
    mixing = block * d_along / jnp.sqrt(bound)
    out_ref[...] = product(mixing, nh[...], nl[...])


def body(initial, cell_matrices, cell_map, face_low, face_high):
    vmem = pl.BlockSpec(memory_space=pltpu.VMEM)
    hbm = pl.BlockSpec(memory_space=pl.ANY)
    dma = pltpu.SemaphoreType.DMA
    half = WIDTH // 2
    return pl.pallas_call(
        kernel,
        out_shape=jax.ShapeDtypeStruct((WIDTH, NODE), f32),
        in_specs=[hbm, hbm, vmem, vmem, vmem],
        out_specs=vmem,
        scratch_shapes=[
            pltpu.VMEM((WIDTH, NODE), f32),
            pltpu.VMEM((NODE, NODE), f32),
            pltpu.VMEM((NODE, NODE), bf16),
            pltpu.VMEM((NODE, NODE), bf16),
            pltpu.VMEM((NODE, NODE), bf16),
            pltpu.VMEM((WIDTH, NODE), f32),
            pltpu.VMEM((WIDTH, NODE), f32),
            pltpu.VMEM((WIDTH, NODE), f32),
            pltpu.VMEM((DEGREE + 1, 2, half, RIM), f32),
            pltpu.VMEM((DEGREE + 1, 2, half, RIM), f32),
            pltpu.VMEM((NORB, NODE), f32),
            pltpu.VMEM((NORB, NODE), bf16),
            pltpu.VMEM((NORB, NODE), bf16),
            pltpu.VMEM((2 * WIDTH, 256), f32),
            pltpu.VMEM((GROUP, 8, 256), f32),
            pltpu.VMEM((FAR, 8, 256), f32),
            pltpu.VMEM((2, NORB, 256), f32),
            pltpu.VMEM((NORB, NORB), bf16),
            pltpu.VMEM((NORB, NORB), bf16),
            pltpu.VMEM((NORB, NORB), f32),
            pltpu.VMEM((NORB, NORB), bf16),
            pltpu.VMEM((NORB, NORB), bf16),
            dma((2,)),
            dma((DEGREE + 1, 2)), dma((DEGREE + 1, 2)),
            dma((14,)), dma((14,)),
            dma((GROUP,)), dma((GROUP,)),
            dma((FAR,)), dma((FAR,)),
            dma((GROUP,)), dma((GROUP,)),
            dma((10,)), dma((10,)),
            pltpu.SemaphoreType.REGULAR((6,)),
        ],
        compiler_params=pltpu.CompilerParams(collective_id=0, has_side_effects=True),
        name="subspace_step",
    )(initial, cell_matrices, cell_map, face_low, face_high)


def solution(mesh):
    placed = (
        P("orb", "cells"),
        P("cells", None, None),
        P("cells", None),
        P("cells", None),
        P("cells", None),
    )
    return jax.shard_map(
        body, mesh=mesh, in_specs=placed, out_specs=P("orb", "cells"), check_vma=False
    )
```

```python
import jax
import jax.numpy as jnp
from jax import lax
from jax.experimental import pallas as pl
from jax.experimental.pallas import tpu as pltpu
from jax.sharding import PartitionSpec as P

DEGREE = 7
NS_ITERS = 3
NODE = 512
FACE = 64
RIM = 2 * FACE
NORB = 512
WIDTH = 64
NX, NY, NZ, NEAR = 4, 4, 32, 4
FAR = NZ // NEAR
GROUP = NY * NEAR
MESH = pl.DeviceIdType.MESH

center_value = 0.6
half_width = 1.6
f32, bf16 = jnp.float32, jnp.bfloat16


def split(a):
    hi = a.astype(bf16)
    return hi, (a - hi.astype(f32)).astype(bf16)


def dot(a, b):
    return jnp.dot(a, b, preferred_element_type=f32)


def dot_t(a, b):
    return lax.dot_general(a, b, (((1,), (1,)), ((), ())), preferred_element_type=f32)


def product(a, b_hi, b_lo, mul=dot):
    hi, lo = split(a)
    rows = a.shape[0]
    both = mul(jnp.concatenate([hi, lo], axis=0), b_hi)
    return both[:rows] + (both[rows:] + mul(hi, b_lo))


def ring_gather(view, c, x, k, ssem, rsem, first, second, passing):
    right_x, left_x = lax.rem(x + 1, NX), lax.rem(x + NX - 1, NX)
    across = lax.rem(x + 2, NX)
    right, left, other = 2 * right_x + k, 2 * left_x + k, 2 * x + (1 - k)

    def send(block, half, slot, target):
        ref = view(block, half)
        copy = pltpu.make_async_remote_copy(
            src_ref=ref, dst_ref=ref, send_sem=ssem.at[slot], recv_sem=rsem.at[slot],
            device_id=(c, target), device_id_type=MESH,
        )
        copy.start()
        return copy

    passed = []

    def pass_over(block, half):
        if half in passing:
            passed.append(send(block, (first, second)[half], 6 + len(passed), other))

    r0 = send(x, first, 0, right)
    l1 = send(x, second, 1, left)
    pass_over(x, 0)
    pass_over(x, 1)
    r1 = send(x, second, 2, right)
    l0 = send(x, first, 3, left)
    r0.wait_recv()
    on = send(left_x, first, 4, right)
    pass_over(left_x, 0)
    l1.wait_recv()
    back = send(right_x, second, 5, left)
    pass_over(right_x, 1)
    r1.wait_recv()
    pass_over(left_x, 1)
    l0.wait_recv()
    pass_over(right_x, 0)
    on.wait_recv()
    pass_over(across, 0)
    back.wait_recv()
    pass_over(across, 1)
    return [r0, l1, r1, l0, on, back], passed


def kernel(
    initial, matrices, cmap_ref, low_ref, high_ref, out_ref,
    init_v, mat_v, q_ref, ah, al, cur, prev, image, sbuf, rbuf,
    block_out, block_in, fbuf, fgot, nbuf, ngot,
    xbuf, nh, nl, cpart, rsbuf, zbuf, corr, th, tl, root, rh, rl,
    load_sem, hs, hr, xs, xr, rs_s, rs_r, z_s, z_r, g_s, g_r, cs, cr,
    bs, br, fs, fr, ns, nr, far_sem,
):
    c = lax.axis_index("cells")
    o = lax.axis_index("orb")
    cells = NY * NZ
    x, k = o // 2, lax.rem(o, 2)
    y, z = c // NZ, lax.rem(c, NZ)
    far, near = z // NEAR, lax.rem(z, NEAR)
    g = y * NEAR + near
    after = lax.rem(c + 1, cells)
    before = lax.rem(c + cells - 1, cells)

    def member(p):
        return (p // NEAR) * NZ + far * NEAR + lax.rem(p, NEAR)

    def distant(q):
        return y * NZ + q * NEAR + near

    load_a = pltpu.make_async_copy(matrices.at[0], mat_v, load_sem.at[0])
    load_x = pltpu.make_async_copy(initial, init_v, load_sem.at[1])
    load_a.start()
    load_x.start()

    barrier = pltpu.get_barrier_semaphore()
    def ring_z(d):
        return (y * NZ + lax.rem(z + d + NZ, NZ), o)

    def ring_y(d):
        return (lax.rem(y + d + NY, NY) * NZ + z, o)

    peers = [ring_z(1), ring_z(-1), ring_y(1), ring_y(-1)]
    peers += [(after, o), (before, o)]
    peers += [
        (c, 2 * lax.rem(x + 1, NX) + k),
        (c, 2 * lax.rem(x + NX - 1, NX) + k),
        (c, 2 * x + (1 - k)),
    ]
    for peer in peers:
        pl.semaphore_signal(barrier, inc=1, device_id=peer, device_id_type=MESH)

    square = (NODE, NODE)
    down = lax.broadcasted_iota(jnp.int32, square, 0).astype(f32)
    along = lax.broadcasted_iota(jnp.int32, square, 1).astype(f32)
    eye64 = lax.broadcasted_iota(jnp.int32, (FACE, FACE), 0) == lax.broadcasted_iota(
        jnp.int32, (FACE, FACE), 1
    )

    def one_hot(mask):
        return jnp.where(mask, 1.0, 0.0).astype(bf16)

    def upright(ref):
        wide = jnp.broadcast_to(ref[...].astype(f32), (FACE, FACE))
        return jnp.sum(jnp.where(eye64, wide, 0.0), axis=1, keepdims=True)

    lanes = lax.broadcasted_iota(jnp.int32, (FACE, NODE), 1).astype(f32)
    ranks = lax.broadcasted_iota(jnp.int32, (FACE, NODE), 0).astype(f32)
    is_low = jnp.where(upright(low_ref) == lanes, 1.0, 0.0)
    is_high = jnp.where(upright(high_ref) == lanes, 1.0, 0.0)
    is_face = jnp.sum(is_low + is_high, axis=0, keepdims=True)
    face_place = jnp.sum(is_low * ranks + is_high * (ranks + FACE), axis=0, keepdims=True)
    others = jnp.broadcast_to(1.0 - is_face, (16, NODE)).astype(bf16)
    rank = dot(others, one_hot(down < along))[0:1]
    place = jnp.where(is_face > 0.5, face_place, rank + RIM)
    q_ref[...] = one_hot(down == place)
    load_x.wait()
    x_hi, x_lo = split(init_v[...])
    x_rest = (init_v[...] - x_hi.astype(f32) - x_lo.astype(f32)).astype(bf16)
    stacked = dot_t(jnp.concatenate([x_hi, x_lo, x_rest], axis=0), q_ref[...])
    cur[...] = stacked[0:64] + (stacked[64:128] + stacked[128:192])
    prev[...] = jnp.zeros_like(prev)

    half = WIDTH // 2
    left_lanes = lax.broadcasted_iota(jnp.int32, (half, RIM), 1) < FACE

    def to_before(rim):
        return jnp.where(left_lanes, rim[:half], pltpu.roll(rim[half:], FACE, 1))

    def to_after(rim):
        return jnp.where(left_lanes, pltpu.roll(rim[:half], FACE, 1), rim[half:])

    def halo_copy(slot, way):
        return pltpu.make_async_remote_copy(
            src_ref=sbuf.at[slot, way], dst_ref=rbuf.at[slot, way],
            send_sem=hs.at[slot, way], recv_sem=hr.at[slot, way],
            device_id=(after if way == 1 else before, o), device_id_type=MESH,
        )

    sbuf[0, 1] = to_after(cur[:, :RIM])
    pl.semaphore_wait(barrier, len(peers))
    start = halo_copy(0, 1)
    start.start()
    stages = [ring_z(1), ring_z(-1)], [ring_z(2), ring_z(-2)], [ring_z(4), ring_z(-4)]
    stages += ([ring_z(8), ring_z(-8)], [ring_y(1), ring_y(-1)], [ring_y(1), ring_y(-1)])
    stages += ([(after, o), (before, o)],)

    def greet(stage):
        for peer in stages[stage]:
            pl.semaphore_signal(far_sem.at[stage], inc=1, device_id=peer, device_id_type=MESH)

    def greeted(stage):
        pl.semaphore_wait(far_sem.at[stage], 2)

    greet(0)
    greet(6)
    cmap = cmap_ref[...].astype(f32)
    at_cell = one_hot(down == cmap)
    upper = jnp.where(place >= 256.0, 1.0, 0.0)
    parts = lax.broadcasted_iota(jnp.int32, (16, NODE), 0)
    coded = jnp.where(
        parts == 0,
        jnp.broadcast_to(upper, (16, NODE)),
        jnp.broadcast_to(place - 256.0 * upper, (16, NODE)),
    ).astype(bf16)
    moved = dot(coded, at_cell)
    cell_place = moved[0:1] * 256.0 + moved[1:2]
    by_cell = one_hot(down == cell_place)
    load_a.wait()
    a_hi, a_lo = split(mat_v[...])
    ah[...] = dot_t(dot(by_cell, a_hi).astype(bf16), by_cell).astype(bf16)
    al[...] = dot_t(dot(by_cell, a_lo).astype(bf16), by_cell).astype(bf16)

    def apply(a, begin, end, first, last):
        hi, lo = split(a)
        rows = slice(begin, end)
        main = dot(jnp.concatenate([hi, lo], axis=0), ah[rows, first:last])
        return main[:WIDTH] + (main[WIDTH:] + dot(hi, al[rows, first:last]))

    def ahead():
        image[...] = apply(cur[:, RIM:], RIM, NODE, 0, NODE)

    block_out[...] = ah[:RIM, :RIM].astype(f32) + al[:RIM, :RIM].astype(f32)

    def neighbour_copy(source, target, send, recv, slot, way, distance):
        to = lax.rem(c + (distance if way == 1 else cells - distance), cells)
        return pltpu.make_async_remote_copy(
            src_ref=source, dst_ref=target, send_sem=send.at[slot, way],
            recv_sem=recv.at[slot, way], device_id=(to, o), device_id_type=MESH,
        )

    blocks = [neighbour_copy(block_out, block_in.at[w], bs, br, 0, w, 1) for w in (0, 1)]
    for copy in blocks:
        copy.start()
    ahead()
    start.wait()
    got = rbuf[0, 1]
    first_rim = cur[:, :RIM]
    cur[:half, :RIM] = jnp.where(left_lanes, got, first_rim[:half])
    cur[half:, :RIM] = jnp.where(left_lanes, pltpu.roll(got, FACE, 1), first_rim[half:])

    def step(index, carry):
        slot = index + 1
        now = cur[:, :RIM]
        rim = image[:, :RIM] + apply(now, 0, RIM, 0, RIM)
        sbuf[slot, 0] = to_before(rim)
        sbuf[slot, 1] = to_after(rim)
        down_copy = halo_copy(slot, 0)
        up_copy = halo_copy(slot, 1)
        down_copy.start()
        up_copy.start()
        greeted(0)
        greet(1)
        factor = 1.0
        inner = image[:, RIM:] + apply(now, 0, RIM, RIM, NODE)
        core = cur[:, RIM:]
        following = factor * (inner - center_value * core) / half_width - prev[:, RIM:]
        prev[:, RIM:] = core
        cur[:, RIM:] = following
        down_copy.wait()
        up_copy.wait()
        from_next = rbuf[slot, 0]
        from_last = rbuf[slot, 1]
        add_top = jnp.where(left_lanes, from_last, pltpu.roll(from_next, FACE, 1))
        add_bottom = jnp.where(left_lanes, pltpu.roll(from_last, FACE, 1), from_next)
        rim = rim + jnp.concatenate([add_top, add_bottom], axis=0)
        edge = factor * (rim - center_value * now) / half_width - prev[:, :RIM]
        prev[:, :RIM] = now
        cur[:, :RIM] = edge
        return carry

    step(0, 0)
    greeted(6)
    for copy in blocks:
        copy.wait()
    wide_left = lax.broadcasted_iota(jnp.int32, (WIDTH, RIM), 1) < FACE
    scale = 2.0 / half_width

    def times_block(a, way):
        b_hi, b_lo = split(block_in[way])
        return product(a, b_hi, b_lo)

    def two_steps(index, carry):
        now, last = cur[...], prev[...]
        image[...] = apply(now, 0, NODE, 0, NODE)
        rim = image[:, :RIM]
        fbuf[index, 0] = to_before(rim)
        fbuf[index, 1] = to_after(rim)
        two = [
            neighbour_copy(fbuf.at[index, w], fgot.at[index, w], fs, fr, index, w, 2) for w in (0, 1)
        ]
        for copy in two:
            copy.start()
        part = scale * (image[...] - center_value * now) - last
        prev[...] = part
        second = apply(part, 0, NODE, 0, RIM)
        turned = pltpu.roll(second, FACE, 1)
        nbuf[index, 0] = jnp.where(wide_left, rim, turned)
        nbuf[index, 1] = jnp.where(wide_left, turned, rim)
        one = [
            neighbour_copy(nbuf.at[index, w], ngot.at[index, w], ns, nr, index, w, 1) for w in (0, 1)
        ]
        for copy in one:
            copy.start()
        for stage in (1, 2, 3):
            @pl.when(index == stage - 1)
            def _():
                greeted(stage)
                greet(stage + 1)
        image[:, :RIM] = second
        image[:, RIM:] = apply(part, 0, NODE, RIM, NODE)
        swapped = pltpu.roll(rim, FACE, 1)
        for copy in two:
            copy.wait()
        far_next = fgot[index, 0]
        far_last = fgot[index, 1]
        to_last = jnp.concatenate([
            jnp.where(left_lanes, far_last, swapped[:half]),
            jnp.where(left_lanes, pltpu.roll(far_last, FACE, 1), swapped[half:]),
        ], axis=0)
        to_next = jnp.concatenate([
            jnp.where(left_lanes, swapped[:half], pltpu.roll(far_next, FACE, 1)),
            jnp.where(left_lanes, swapped[half:], far_next),
        ], axis=0)
        through = jnp.where(wide_left, times_block(to_next, 0), times_block(to_last, 1))
        through = scale * pltpu.roll(through, FACE, 1)
        for copy in one:
            copy.wait()
        from_next = ngot[index, 0]
        from_last = ngot[index, 1]
        received = scale * pltpu.roll(jnp.where(wide_left, from_next, from_last), FACE, 1)
        later = jnp.where(wide_left, from_last, from_next) + through
        image[...] = image[...] + apply(received, 0, RIM, 0, NODE)
        image[:, :RIM] = image[:, :RIM] + later
        prev[:, :RIM] = prev[:, :RIM] + received
        cur[...] = scale * (image[...] - center_value * prev[...]) - now
        return carry

    lax.fori_loop(0, (DEGREE - 1) // 2, two_steps, 0)
    greeted(4)
    greet(5)

    mine = (k * NX + x) * WIDTH

    def orbitals(block, part):
        start = (k * NX + block) * WIDTH + part * half
        return xbuf.at[pl.ds(pl.multiple_of(start, half), half), :]

    xbuf[pl.ds(pl.multiple_of(mine, WIDTH), WIDTH), :] = cur[...]
    x_sent, x_passed = ring_gather(orbitals, c, x, k, xs, xr, 0, 1, (0, 1))
    greeted(5)
    for copy in x_passed[:2]:
        copy.wait_recv()

    side = pl.ds(pl.multiple_of(k * 256, 256), 256)
    e_hi, e_lo = split(xbuf[side, :])
    owned = lax.broadcasted_iota(jnp.int32, (2 * WIDTH, NODE), 1) >= FACE
    chip = jnp.concatenate(
        [xbuf[pl.ds(pl.multiple_of(b * 256 + x * WIDTH, WIDTH), WIDTH), :] for b in (0, 1)], axis=0
    )
    cpart[...] = product(jnp.where(owned, chip, 0.0), e_hi, e_lo, dot_t)

    def slab(p):
        row = (p // 8) * 256 + x * WIDTH + lax.rem(p, 8) * 8
        return pl.ds(pl.multiple_of(row, 8), 8)

    own_slab = pl.ds(pl.multiple_of(g * 8, 8), 8)
    shares = []
    for d in range(1, GROUP):
        p = lax.rem(g + d, GROUP)
        copy = pltpu.make_async_remote_copy(
            src_ref=cpart.at[pl.ds(pl.multiple_of(p * 8, 8), 8), :], dst_ref=rsbuf.at[g],
            send_sem=rs_s.at[d], recv_sem=rs_r.at[d],
            device_id=(member(p), o), device_id_type=MESH,
        )
        copy.start()
        shares.append(copy)
    rsbuf[g] = cpart[own_slab, :]
    for copy in shares:
        copy.wait_recv()
    zbuf[far] = jnp.sum(rsbuf[...], axis=0)
    sums = []
    for d in (4, 3, 5, 2, 6, 1, 7):
        copy = pltpu.make_async_remote_copy(
            src_ref=zbuf.at[far], dst_ref=zbuf.at[far],
            send_sem=z_s.at[d], recv_sem=z_r.at[d],
            device_id=(distant(lax.rem(far + d, FAR)), o), device_id_type=MESH,
        )
        copy.start()
        sums.append(copy)
    for copy in x_passed[2:]:
        copy.wait_recv()
    e_hi, e_lo = split(xbuf[...])
    nh[...] = dot(e_hi, q_ref[...]).astype(bf16)
    nl[...] = dot(e_lo, q_ref[...]).astype(bf16)
    for copy in shares + x_sent + x_passed:
        copy.wait_send()
    for copy in sums:
        copy.wait_recv()
    total = jnp.sum(zbuf[...], axis=0) / float(cells * (NODE - FACE))
    corr[k, slab(g)] = total
    spread = []
    for d in range(1, GROUP):
        ref = corr.at[k, slab(g)]
        copy = pltpu.make_async_remote_copy(
            src_ref=ref, dst_ref=ref, send_sem=g_s.at[d], recv_sem=g_r.at[d],
            device_id=(member(lax.rem(g + d, GROUP)), o), device_id_type=MESH,
        )
        copy.start()
        spread.append(copy)
    for copy in sums:
        copy.wait_send()
    for copy in spread:
        copy.wait_recv()
    for copy in spread:
        copy.wait_send()

    def quarter(block, part):
        return corr.at[k, pl.ds(pl.multiple_of(part * 256 + block * WIDTH, WIDTH), WIDTH)]

    c_sent, c_passed = ring_gather(quarter, c, x, k, cs, cr, k, 1 - k, (0,))
    off_side = pl.ds(pl.multiple_of((1 - k) * 256, 256), 256)
    corr[1 - k, side] = corr[k, off_side].T
    for copy in c_passed:
        copy.wait_recv()
    for copy in c_sent + c_passed:
        copy.wait_send()

    full = jnp.concatenate([corr[0], corr[1]], axis=1)
    diagonal = jnp.where(down == along, full, 0.0)
    d_along = 1.0 / jnp.sqrt(jnp.sum(diagonal, axis=0, keepdims=True))
    d_down = 1.0 / jnp.sqrt(jnp.sum(diagonal, axis=1, keepdims=True))
    scaled = full * d_down * d_along
    bound = jnp.max(jnp.sum(jnp.abs(scaled), axis=1, keepdims=True), axis=0, keepdims=True)
    target = scaled / bound
    hi, lo = split(target)
    th[...] = hi
    tl[...] = lo
    root[...] = 0.5 * (jnp.where(down == along, 3.0, 0.0) - target)
    for iteration in range(NS_ITERS - 2):
        hi, lo = split(root[...])
        rh[...] = hi
        rl[...] = lo
        inner = product(root[...], rh[...], rl[...])
        in_hi, in_lo = split(inner)
        inner = product(target, in_hi, in_lo)
        in_hi, in_lo = split(inner)
        inner = product(root[...], in_hi, in_lo)
        root[...] = 0.5 * (3.0 * root[...] - inner)
    hi, lo = split(root[...])
    rh[...] = hi
    rl[...] = lo
    block = root[pl.ds(pl.multiple_of(mine, WIDTH), WIDTH), :]
    inner = product(block, rh[...], rl[...])
    inner = product(inner, th[...], tl[...])
    inner = product(inner, rh[...], rl[...])
    block = 0.5 * (3.0 * block - inner)
    mixing = block * d_along / jnp.sqrt(bound)
    out_ref[...] = product(mixing, nh[...], nl[...])


def body(initial, cell_matrices, cell_map, face_low, face_high):
    vmem = pl.BlockSpec(memory_space=pltpu.VMEM)
    hbm = pl.BlockSpec(memory_space=pl.ANY)
    dma = pltpu.SemaphoreType.DMA
    half = WIDTH // 2
    return pl.pallas_call(
        kernel,
        out_shape=jax.ShapeDtypeStruct((WIDTH, NODE), f32),
        in_specs=[hbm, hbm, vmem, vmem, vmem],
        out_specs=vmem,
        scratch_shapes=[
            pltpu.VMEM((WIDTH, NODE), f32),
            pltpu.VMEM((NODE, NODE), f32),
            pltpu.VMEM((NODE, NODE), bf16),
            pltpu.VMEM((NODE, NODE), bf16),
            pltpu.VMEM((NODE, NODE), bf16),
            pltpu.VMEM((WIDTH, NODE), f32),
            pltpu.VMEM((WIDTH, NODE), f32),
            pltpu.VMEM((WIDTH, NODE), f32),
            pltpu.VMEM((2, 2, half, RIM), f32),
            pltpu.VMEM((2, 2, half, RIM), f32),
            pltpu.VMEM((RIM, RIM), f32),
            pltpu.VMEM((2, RIM, RIM), f32),
            pltpu.VMEM((DEGREE // 2, 2, half, RIM), f32),
            pltpu.VMEM((DEGREE // 2, 2, half, RIM), f32),
            pltpu.VMEM((DEGREE // 2, 2, WIDTH, RIM), f32),
            pltpu.VMEM((DEGREE // 2, 2, WIDTH, RIM), f32),
            pltpu.VMEM((NORB, NODE), f32),
            pltpu.VMEM((NORB, NODE), bf16),
            pltpu.VMEM((NORB, NODE), bf16),
            pltpu.VMEM((2 * WIDTH, 256), f32),
            pltpu.VMEM((GROUP, 8, 256), f32),
            pltpu.VMEM((FAR, 8, 256), f32),
            pltpu.VMEM((2, NORB, 256), f32),
            pltpu.VMEM((NORB, NORB), bf16),
            pltpu.VMEM((NORB, NORB), bf16),
            pltpu.VMEM((NORB, NORB), f32),
            pltpu.VMEM((NORB, NORB), bf16),
            pltpu.VMEM((NORB, NORB), bf16),
            dma((2,)),
            dma((2, 2)), dma((2, 2)),
            dma((14,)), dma((14,)),
            dma((GROUP,)), dma((GROUP,)),
            dma((FAR,)), dma((FAR,)),
            dma((GROUP,)), dma((GROUP,)),
            dma((10,)), dma((10,)),
            dma((1, 2)), dma((1, 2)),
            dma((DEGREE // 2, 2)), dma((DEGREE // 2, 2)),
            dma((DEGREE // 2, 2)), dma((DEGREE // 2, 2)),
            pltpu.SemaphoreType.REGULAR((7,)),
        ],
        compiler_params=pltpu.CompilerParams(collective_id=0, has_side_effects=True),
        name="subspace_step",
    )(initial, cell_matrices, cell_map, face_low, face_high)


def solution(mesh):
    placed = (
        P("orb", "cells"),
        P("cells", None, None),
        P("cells", None),
        P("cells", None),
        P("cells", None),
    )
    return jax.shard_map(
        body, mesh=mesh, in_specs=placed, out_specs=P("orb", "cells"), check_vma=False
    )
```

```python
import jax
import jax.numpy as jnp
from jax import lax
from jax.experimental import pallas as pl
from jax.experimental.pallas import tpu as pltpu
from jax.sharding import PartitionSpec as P

DEGREE = 7
NS_ITERS = 3
NODE = 512
FACE = 64
RIM = 2 * FACE
NORB = 512
WIDTH = 64
NX, NY, NZ, NEAR = 4, 4, 32, 4
FAR = NZ // NEAR
GROUP = NY * NEAR
MESH = pl.DeviceIdType.MESH

center_value = 0.6
half_width = 1.6
f32, bf16 = jnp.float32, jnp.bfloat16


def split(a):
    hi = a.astype(bf16)
    return hi, (a - hi.astype(f32)).astype(bf16)


def dot(a, b):
    return jnp.dot(a, b, preferred_element_type=f32)


def dot_t(a, b):
    return lax.dot_general(a, b, (((1,), (1,)), ((), ())), preferred_element_type=f32)


def product(a, b_hi, b_lo, mul=dot):
    hi, lo = split(a)
    rows = a.shape[0]
    both = mul(jnp.concatenate([hi, lo], axis=0), b_hi)
    return both[:rows] + (both[rows:] + mul(hi, b_lo))


def ring_gather(view, c, x, k, ssem, rsem, first, second, passing):
    right_x, left_x = lax.rem(x + 1, NX), lax.rem(x + NX - 1, NX)
    across = lax.rem(x + 2, NX)
    right, left, other = 2 * right_x + k, 2 * left_x + k, 2 * x + (1 - k)

    def send(block, half, slot, target):
        ref = view(block, half)
        copy = pltpu.make_async_remote_copy(
            src_ref=ref, dst_ref=ref, send_sem=ssem.at[slot], recv_sem=rsem.at[slot],
            device_id=(c, target), device_id_type=MESH,
        )
        copy.start()
        return copy

    passed = []

    def pass_over(block, half):
        if half in passing:
            passed.append(send(block, (first, second)[half], 6 + len(passed), other))

    r0 = send(x, first, 0, right)
    l1 = send(x, second, 1, left)
    pass_over(x, 0)
    pass_over(x, 1)
    r1 = send(x, second, 2, right)
    l0 = send(x, first, 3, left)
    r0.wait_recv()
    on = send(left_x, first, 4, right)
    pass_over(left_x, 0)
    l1.wait_recv()
    back = send(right_x, second, 5, left)
    pass_over(right_x, 1)
    r1.wait_recv()
    pass_over(left_x, 1)
    l0.wait_recv()
    pass_over(right_x, 0)
    on.wait_recv()
    pass_over(across, 0)
    back.wait_recv()
    pass_over(across, 1)
    return [r0, l1, r1, l0, on, back], passed


def kernel(
    initial, matrices, cmap_ref, low_ref, high_ref, out_ref,
    init_v, mat_v, q_ref, ah, al, cur, prev, image, sbuf, rbuf,
    block_out, block_in, fbuf, fgot, nbuf, ngot,
    xbuf, nh, nl, cpart, rsbuf, zbuf, corr, th, tl, root, rh, rl,
    load_sem, hs, hr, xs, xr, rs_s, rs_r, z_s, z_r, g_s, g_r, cs, cr,
    bs, br, fs, fr, ns, nr, far_sem,
):
    c = lax.axis_index("cells")
    o = lax.axis_index("orb")
    cells = NY * NZ
    x, k = o // 2, lax.rem(o, 2)
    y, z = c // NZ, lax.rem(c, NZ)
    far, near = z // NEAR, lax.rem(z, NEAR)
    g = y * NEAR + near
    after = lax.rem(c + 1, cells)
    before = lax.rem(c + cells - 1, cells)

    def member(p):
        return (p // NEAR) * NZ + far * NEAR + lax.rem(p, NEAR)

    def distant(q):
        return y * NZ + q * NEAR + near

    load_a = pltpu.make_async_copy(matrices.at[0], mat_v, load_sem.at[0])
    load_x = pltpu.make_async_copy(initial, init_v, load_sem.at[1])
    load_a.start()
    load_x.start()

    barrier = pltpu.get_barrier_semaphore()
    def ring_z(d):
        return (y * NZ + lax.rem(z + d + NZ, NZ), o)

    def ring_y(d):
        return (lax.rem(y + d + NY, NY) * NZ + z, o)

    peers = [ring_z(1), ring_z(-1), ring_y(1), ring_y(-1)]
    peers += [(after, o), (before, o)]
    peers += [
        (c, 2 * lax.rem(x + 1, NX) + k),
        (c, 2 * lax.rem(x + NX - 1, NX) + k),
        (c, 2 * x + (1 - k)),
    ]
    for peer in peers:
        pl.semaphore_signal(barrier, inc=1, device_id=peer, device_id_type=MESH)

    square = (NODE, NODE)
    down = lax.broadcasted_iota(jnp.int32, square, 0).astype(f32)
    along = lax.broadcasted_iota(jnp.int32, square, 1).astype(f32)
    eye64 = lax.broadcasted_iota(jnp.int32, (FACE, FACE), 0) == lax.broadcasted_iota(
        jnp.int32, (FACE, FACE), 1
    )

    def one_hot(mask):
        return jnp.where(mask, 1.0, 0.0).astype(bf16)

    def upright(ref):
        wide = jnp.broadcast_to(ref[...].astype(f32), (FACE, FACE))
        return jnp.sum(jnp.where(eye64, wide, 0.0), axis=1, keepdims=True)

    lanes = lax.broadcasted_iota(jnp.int32, (FACE, NODE), 1).astype(f32)
    ranks = lax.broadcasted_iota(jnp.int32, (FACE, NODE), 0).astype(f32)
    is_low = jnp.where(upright(low_ref) == lanes, 1.0, 0.0)
    is_high = jnp.where(upright(high_ref) == lanes, 1.0, 0.0)
    is_face = jnp.sum(is_low + is_high, axis=0, keepdims=True)
    face_place = jnp.sum(is_low * ranks + is_high * (ranks + FACE), axis=0, keepdims=True)
    others = jnp.broadcast_to(1.0 - is_face, (16, NODE)).astype(bf16)
    rank = dot(others, one_hot(down < along))[0:1]
    place = jnp.where(is_face > 0.5, face_place, rank + RIM)
    q_ref[...] = one_hot(down == place)
    load_x.wait()
    x_hi, x_lo = split(init_v[...])
    x_rest = (init_v[...] - x_hi.astype(f32) - x_lo.astype(f32)).astype(bf16)
    stacked = dot_t(jnp.concatenate([x_hi, x_lo, x_rest], axis=0), q_ref[...])
    cur[...] = stacked[0:64] + (stacked[64:128] + stacked[128:192])
    prev[...] = jnp.zeros_like(prev)

    half = WIDTH // 2
    left_lanes = lax.broadcasted_iota(jnp.int32, (half, RIM), 1) < FACE

    def to_before(rim):
        return jnp.where(left_lanes, rim[:half], pltpu.roll(rim[half:], FACE, 1))

    def to_after(rim):
        return jnp.where(left_lanes, pltpu.roll(rim[:half], FACE, 1), rim[half:])

    def halo_copy(slot, way):
        return pltpu.make_async_remote_copy(
            src_ref=sbuf.at[slot, way], dst_ref=rbuf.at[slot, way],
            send_sem=hs.at[slot, way], recv_sem=hr.at[slot, way],
            device_id=(after if way == 1 else before, o), device_id_type=MESH,
        )

    sbuf[0, 1] = to_after(cur[:, :RIM])
    pl.semaphore_wait(barrier, len(peers))
    start = halo_copy(0, 1)
    start.start()
    stages = [ring_z(1), ring_z(-1)], [ring_z(2), ring_z(-2)], [ring_z(4), ring_z(-4)]
    stages += ([ring_z(8), ring_z(-8)], [ring_y(1), ring_y(-1)], [ring_y(1), ring_y(-1)])
    stages += ([(after, o), (before, o)],)

    def greet(stage):
        for peer in stages[stage]:
            pl.semaphore_signal(far_sem.at[stage], inc=1, device_id=peer, device_id_type=MESH)

    def greeted(stage):
        pl.semaphore_wait(far_sem.at[stage], 2)

    greet(0)
    greet(6)
    cmap = cmap_ref[...].astype(f32)
    at_cell = one_hot(down == cmap)
    upper = jnp.where(place >= 256.0, 1.0, 0.0)
    parts = lax.broadcasted_iota(jnp.int32, (16, NODE), 0)
    coded = jnp.where(
        parts == 0,
        jnp.broadcast_to(upper, (16, NODE)),
        jnp.broadcast_to(place - 256.0 * upper, (16, NODE)),
    ).astype(bf16)
    moved = dot(coded, at_cell)
    cell_place = moved[0:1] * 256.0 + moved[1:2]
    by_cell = one_hot(down == cell_place)
    load_a.wait()
    a_hi, a_lo = split(mat_v[...])
    ah[...] = dot_t(dot(by_cell, a_hi).astype(bf16), by_cell).astype(bf16)
    al[...] = dot_t(dot(by_cell, a_lo).astype(bf16), by_cell).astype(bf16)

    def apply(a, begin, end, first, last):
        hi, lo = split(a)
        rows = slice(begin, end)
        main = dot(jnp.concatenate([hi, lo], axis=0), ah[rows, first:last])
        return main[:WIDTH] + (main[WIDTH:] + dot(hi, al[rows, first:last]))

    def neighbour_copy(source, target, send, recv, slot, way, distance):
        to = lax.rem(c + (distance if way == 1 else cells - distance), cells)
        return pltpu.make_async_remote_copy(
            src_ref=source, dst_ref=target, send_sem=send.at[slot, way],
            recv_sem=recv.at[slot, way], device_id=(to, o), device_id_type=MESH,
        )

    blocks = [neighbour_copy(block_out, block_in.at[w], bs, br, 0, w, 1) for w in (0, 1)]
    image[:, :RIM] = apply(cur[:, RIM:], RIM, NODE, 0, RIM)
    start.wait()
    got = rbuf[0, 1]
    first_rim = cur[:, :RIM]
    cur[:half, :RIM] = jnp.where(left_lanes, got, first_rim[:half])
    cur[half:, :RIM] = jnp.where(left_lanes, pltpu.roll(got, FACE, 1), first_rim[half:])

    def step(index, carry):
        slot = index + 1
        now = cur[:, :RIM]
        rim = image[:, :RIM] + apply(now, 0, RIM, 0, RIM)
        sbuf[slot, 0] = to_before(rim)
        sbuf[slot, 1] = to_after(rim)
        down_copy = halo_copy(slot, 0)
        up_copy = halo_copy(slot, 1)
        down_copy.start()
        up_copy.start()
        block_out[...] = ah[:RIM, :RIM].astype(f32) + al[:RIM, :RIM].astype(f32)
        for copy in blocks:
            copy.start()
        greeted(0)
        greet(1)
        factor = 1.0
        inner = apply(cur[:, RIM:], RIM, NODE, RIM, NODE) + apply(now, 0, RIM, RIM, NODE)
        core = cur[:, RIM:]
        following = factor * (inner - center_value * core) / half_width - prev[:, RIM:]
        prev[:, RIM:] = core
        cur[:, RIM:] = following
        down_copy.wait()
        up_copy.wait()
        from_next = rbuf[slot, 0]
        from_last = rbuf[slot, 1]
        add_top = jnp.where(left_lanes, from_last, pltpu.roll(from_next, FACE, 1))
        add_bottom = jnp.where(left_lanes, pltpu.roll(from_last, FACE, 1), from_next)
        rim = rim + jnp.concatenate([add_top, add_bottom], axis=0)
        edge = factor * (rim - center_value * now) / half_width - prev[:, :RIM]
        prev[:, :RIM] = now
        cur[:, :RIM] = edge
        return carry

    step(0, 0)
    greeted(6)
    for copy in blocks:
        copy.wait()
    wide_left = lax.broadcasted_iota(jnp.int32, (WIDTH, RIM), 1) < FACE
    scale = 2.0 / half_width

    def times_block(a, way):
        b_hi, b_lo = split(block_in[way])
        return product(a, b_hi, b_lo)

    def two_steps(index, carry):
        now, last = cur[...], prev[...]
        image[...] = apply(now, 0, NODE, 0, NODE)
        rim = image[:, :RIM]
        fbuf[index, 0] = to_before(rim)
        fbuf[index, 1] = to_after(rim)
        two = [
            neighbour_copy(fbuf.at[index, w], fgot.at[index, w], fs, fr, index, w, 2) for w in (0, 1)
        ]
        for copy in two:
            copy.start()
        part = scale * (image[...] - center_value * now) - last
        prev[...] = part
        second = apply(part, 0, NODE, 0, RIM)
        turned = pltpu.roll(second, FACE, 1)
        nbuf[index, 0] = jnp.where(wide_left, rim, turned)
        nbuf[index, 1] = jnp.where(wide_left, turned, rim)
        one = [
            neighbour_copy(nbuf.at[index, w], ngot.at[index, w], ns, nr, index, w, 1) for w in (0, 1)
        ]
        for copy in one:
            copy.start()
        for stage in (1, 2, 3):
            @pl.when(index == stage - 1)
            def _():
                greeted(stage)
                greet(stage + 1)
        image[:, :RIM] = second
        image[:, RIM:] = apply(part, 0, NODE, RIM, NODE)
        swapped = pltpu.roll(rim, FACE, 1)
        for copy in two:
            copy.wait()
        far_next = fgot[index, 0]
        far_last = fgot[index, 1]
        to_last = jnp.concatenate([
            jnp.where(left_lanes, far_last, swapped[:half]),
            jnp.where(left_lanes, pltpu.roll(far_last, FACE, 1), swapped[half:]),
        ], axis=0)
        to_next = jnp.concatenate([
            jnp.where(left_lanes, swapped[:half], pltpu.roll(far_next, FACE, 1)),
            jnp.where(left_lanes, swapped[half:], far_next),
        ], axis=0)
        through = jnp.where(wide_left, times_block(to_next, 0), times_block(to_last, 1))
        through = scale * pltpu.roll(through, FACE, 1)
        for copy in one:
            copy.wait()
        from_next = ngot[index, 0]
        from_last = ngot[index, 1]
        received = scale * pltpu.roll(jnp.where(wide_left, from_next, from_last), FACE, 1)
        later = jnp.where(wide_left, from_last, from_next) + through
        image[...] = image[...] + apply(received, 0, RIM, 0, NODE)
        image[:, :RIM] = image[:, :RIM] + later
        prev[:, :RIM] = prev[:, :RIM] + received
        cur[...] = scale * (image[...] - center_value * prev[...]) - now
        return carry

    lax.fori_loop(0, (DEGREE - 1) // 2, two_steps, 0)
    greeted(4)
    greet(5)

    mine = (k * NX + x) * WIDTH

    def orbitals(block, part):
        start = (k * NX + block) * WIDTH + part * half
        return xbuf.at[pl.ds(pl.multiple_of(start, half), half), :]

    xbuf[pl.ds(pl.multiple_of(mine, WIDTH), WIDTH), :] = cur[...]
    x_sent, x_passed = ring_gather(orbitals, c, x, k, xs, xr, 0, 1, (0, 1))
    greeted(5)
    for copy in x_passed[:2]:
        copy.wait_recv()

    side = pl.ds(pl.multiple_of(k * 256, 256), 256)
    e_hi, e_lo = split(xbuf[side, :])
    owned = lax.broadcasted_iota(jnp.int32, (2 * WIDTH, NODE), 1) >= FACE
    chip = jnp.concatenate(
        [xbuf[pl.ds(pl.multiple_of(b * 256 + x * WIDTH, WIDTH), WIDTH), :] for b in (0, 1)], axis=0
    )
    cpart[...] = product(jnp.where(owned, chip, 0.0), e_hi, e_lo, dot_t)

    def slab(p):
        row = (p // 8) * 256 + x * WIDTH + lax.rem(p, 8) * 8
        return pl.ds(pl.multiple_of(row, 8), 8)

    own_slab = pl.ds(pl.multiple_of(g * 8, 8), 8)
    shares = []
    for d in range(1, GROUP):
        p = lax.rem(g + d, GROUP)
        copy = pltpu.make_async_remote_copy(
            src_ref=cpart.at[pl.ds(pl.multiple_of(p * 8, 8), 8), :], dst_ref=rsbuf.at[g],
            send_sem=rs_s.at[d], recv_sem=rs_r.at[d],
            device_id=(member(p), o), device_id_type=MESH,
        )
        copy.start()
        shares.append(copy)
    rsbuf[g] = cpart[own_slab, :]
    for copy in shares:
        copy.wait_recv()
    zbuf[far] = jnp.sum(rsbuf[...], axis=0)
    sums = []
    for d in (4, 3, 5, 2, 6, 1, 7):
        copy = pltpu.make_async_remote_copy(
            src_ref=zbuf.at[far], dst_ref=zbuf.at[far],
            send_sem=z_s.at[d], recv_sem=z_r.at[d],
            device_id=(distant(lax.rem(far + d, FAR)), o), device_id_type=MESH,
        )
        copy.start()
        sums.append(copy)
    for copy in x_passed[2:]:
        copy.wait_recv()
    e_hi, e_lo = split(xbuf[...])
    nh[...] = dot(e_hi, q_ref[...]).astype(bf16)
    nl[...] = dot(e_lo, q_ref[...]).astype(bf16)
    for copy in shares + x_sent + x_passed:
        copy.wait_send()
    for copy in sums:
        copy.wait_recv()
    total = jnp.sum(zbuf[...], axis=0) / float(cells * (NODE - FACE))
    corr[k, slab(g)] = total
    spread = []
    for d in range(1, GROUP):
        ref = corr.at[k, slab(g)]
        copy = pltpu.make_async_remote_copy(
            src_ref=ref, dst_ref=ref, send_sem=g_s.at[d], recv_sem=g_r.at[d],
            device_id=(member(lax.rem(g + d, GROUP)), o), device_id_type=MESH,
        )
        copy.start()
        spread.append(copy)
    for copy in sums:
        copy.wait_send()
    for copy in spread:
        copy.wait_recv()
    for copy in spread:
        copy.wait_send()

    def quarter(block, part):
        return corr.at[k, pl.ds(pl.multiple_of(part * 256 + block * WIDTH, WIDTH), WIDTH)]

    c_sent, c_passed = ring_gather(quarter, c, x, k, cs, cr, k, 1 - k, (0,))
    off_side = pl.ds(pl.multiple_of((1 - k) * 256, 256), 256)
    corr[1 - k, side] = corr[k, off_side].T
    for copy in c_passed:
        copy.wait_recv()
    for copy in c_sent + c_passed:
        copy.wait_send()

    full = jnp.concatenate([corr[0], corr[1]], axis=1)
    diagonal = jnp.where(down == along, full, 0.0)
    d_along = 1.0 / jnp.sqrt(jnp.sum(diagonal, axis=0, keepdims=True))
    d_down = 1.0 / jnp.sqrt(jnp.sum(diagonal, axis=1, keepdims=True))
    scaled = full * d_down * d_along
    bound = jnp.max(jnp.sum(jnp.abs(scaled), axis=1, keepdims=True), axis=0, keepdims=True)
    target = scaled / bound
    hi, lo = split(target)
    th[...] = hi
    tl[...] = lo
    root[...] = 0.5 * (jnp.where(down == along, 3.0, 0.0) - target)
    for iteration in range(NS_ITERS - 2):
        hi, lo = split(root[...])
        rh[...] = hi
        rl[...] = lo
        inner = product(root[...], rh[...], rl[...])
        in_hi, in_lo = split(inner)
        inner = product(target, in_hi, in_lo)
        in_hi, in_lo = split(inner)
        inner = product(root[...], in_hi, in_lo)
        root[...] = 0.5 * (3.0 * root[...] - inner)
    hi, lo = split(root[...])
    rh[...] = hi
    rl[...] = lo
    block = root[pl.ds(pl.multiple_of(mine, WIDTH), WIDTH), :]
    inner = product(block, rh[...], rl[...])
    inner = product(inner, th[...], tl[...])
    inner = product(inner, rh[...], rl[...])
    block = 0.5 * (3.0 * block - inner)
    mixing = block * d_along / jnp.sqrt(bound)
    out_ref[...] = product(mixing, nh[...], nl[...])


def body(initial, cell_matrices, cell_map, face_low, face_high):
    vmem = pl.BlockSpec(memory_space=pltpu.VMEM)
    hbm = pl.BlockSpec(memory_space=pl.ANY)
    dma = pltpu.SemaphoreType.DMA
    half = WIDTH // 2
    return pl.pallas_call(
        kernel,
        out_shape=jax.ShapeDtypeStruct((WIDTH, NODE), f32),
        in_specs=[hbm, hbm, vmem, vmem, vmem],
        out_specs=vmem,
        scratch_shapes=[
            pltpu.VMEM((WIDTH, NODE), f32),
            pltpu.VMEM((NODE, NODE), f32),
            pltpu.VMEM((NODE, NODE), bf16),
            pltpu.VMEM((NODE, NODE), bf16),
            pltpu.VMEM((NODE, NODE), bf16),
            pltpu.VMEM((WIDTH, NODE), f32),
            pltpu.VMEM((WIDTH, NODE), f32),
            pltpu.VMEM((WIDTH, NODE), f32),
            pltpu.VMEM((2, 2, half, RIM), f32),
            pltpu.VMEM((2, 2, half, RIM), f32),
            pltpu.VMEM((RIM, RIM), f32),
            pltpu.VMEM((2, RIM, RIM), f32),
            pltpu.VMEM((DEGREE // 2, 2, half, RIM), f32),
            pltpu.VMEM((DEGREE // 2, 2, half, RIM), f32),
            pltpu.VMEM((DEGREE // 2, 2, WIDTH, RIM), f32),
            pltpu.VMEM((DEGREE // 2, 2, WIDTH, RIM), f32),
            pltpu.VMEM((NORB, NODE), f32),
            pltpu.VMEM((NORB, NODE), bf16),
            pltpu.VMEM((NORB, NODE), bf16),
            pltpu.VMEM((2 * WIDTH, 256), f32),
            pltpu.VMEM((GROUP, 8, 256), f32),
            pltpu.VMEM((FAR, 8, 256), f32),
            pltpu.VMEM((2, NORB, 256), f32),
            pltpu.VMEM((NORB, NORB), bf16),
            pltpu.VMEM((NORB, NORB), bf16),
            pltpu.VMEM((NORB, NORB), f32),
            pltpu.VMEM((NORB, NORB), bf16),
            pltpu.VMEM((NORB, NORB), bf16),
            dma((2,)),
            dma((2, 2)), dma((2, 2)),
            dma((14,)), dma((14,)),
            dma((GROUP,)), dma((GROUP,)),
            dma((FAR,)), dma((FAR,)),
            dma((GROUP,)), dma((GROUP,)),
            dma((10,)), dma((10,)),
            dma((1, 2)), dma((1, 2)),
            dma((DEGREE // 2, 2)), dma((DEGREE // 2, 2)),
            dma((DEGREE // 2, 2)), dma((DEGREE // 2, 2)),
            pltpu.SemaphoreType.REGULAR((7,)),
        ],
        compiler_params=pltpu.CompilerParams(collective_id=0, has_side_effects=True),
        name="subspace_step",
    )(initial, cell_matrices, cell_map, face_low, face_high)


def solution(mesh):
    placed = (
        P("orb", "cells"),
        P("cells", None, None),
        P("cells", None),
        P("cells", None),
        P("cells", None),
    )
    return jax.shard_map(
        body, mesh=mesh, in_specs=placed, out_specs=P("orb", "cells"), check_vma=False
    )
```
